512 devices in a mesh: gx: 32 (over z, core), gy: 16 (over y, x).
Axes of the slice: x: 4, y: 4, z: 16, core: 2. Of those that a mesh axis runs over, the one named last changes fastest.
Arguments:
- positions: float32 [3, 32768], P(None, ('gx', 'gy')), may hold values from -6 to 6
- block_prev: float32 [32, 3, 32768], P(None, None, ('gx', 'gy')), may hold values from -6 to 6
- block_cur: float32 [32, 3, 32768], P(None, None, ('gx', 'gy')), may hold values from -6 to 6
- neighbours: int32 [32, 32768], P(None, ('gx', 'gy')), may hold values from 0 to 319
- counts: int32 [32768], P(('gx', 'gy')), may hold values from 1 to 32
- x_lists: int32 [512, 2, 64], P(('gx', 'gy')), may hold values from 0 to 63, as said below
- y_lists: int32 [512, 2, 64], P(('gx', 'gy')), may hold values from 0 to 191, as said below
- w_radial: float32 [8, 128], replicated, may hold values from -0.375 to 0.375
- w_vector: float32 [8, 128], replicated, may hold values from -1.5 to 1.5
- w_mix: float32 [128, 128], replicated, may hold values from -0.5 to 0.5
- w_out: float32 [128], replicated, may hold values from -0.5 to 0.5
Outputs:
- new_blocks: float32 [2, 32, 3, 32768], P(None, None, None, ('gx', 'gy'))
- factors: float32 [2, 32, 32], replicated
The draws below stay inside these ranges and needn't reach their ends.
Inputs may be any that keep to these rules, and one draw needn't show every extreme that they name: `x_lists`: the two lists of a domain each hold distinct indices of the domain's own atoms. `y_lists`: the two lists of a domain each hold distinct indices into the domain's widened atoms (own atoms, then the two received gx lists).
All inputs are finite; a program needn't handle non-finite values.
Results may differ from the reference program's by a relative error of at most 0.0003.
Values sent between devices are 32-bit elements; how exact they have to be, the bound alone decides.
A program may use at most 64 MiB of HBM per device.

```python
import jax
import jax.numpy as jnp
from jax import lax

VECTORS = 32
CHANNELS = 128
BASIS_SIZE = 8
SLOT_COUNT = 32
LANCZOS_STEPS = 2
ATOMS_DEV = 64
HALO_ATOMS = 64
EXTENDED = 320
DOMAINS = 512
ATOM_TOTAL = 32768
N_GX = 32
N_GY = 16


def draw_x_lists(key, part):
    subkeys = jax.random.split(jax.random.fold_in(key, 11), DOMAINS * 2)
    picked = jax.vmap(lambda subkey: jax.random.permutation(subkey, ATOMS_DEV)[:HALO_ATOMS])(subkeys)
    return picked.reshape(DOMAINS, 2, HALO_ATOMS).astype(jnp.int32)


def draw_y_lists(key, part):
    subkeys = jax.random.split(jax.random.fold_in(key, 23), DOMAINS * 2)
    picked = jax.vmap(lambda subkey: jax.random.permutation(subkey, ATOMS_DEV + 2 * HALO_ATOMS)[:HALO_ATOMS])(subkeys)
    return picked.reshape(DOMAINS, 2, HALO_ATOMS).astype(jnp.int32)


def set_ends(values, key, least, largest):
    dims = values.shape
    index_at = [jax.random.randint(jax.random.fold_in(key, axis), (), 0, dims[axis]) for axis in range(len(dims))]
    values = values.at[tuple(index_at)].set(least)
    longest = dims.index(max(dims))
    index_at[longest] = (index_at[longest] + 1) % dims[longest]
    return values.at[tuple(index_at)].set(largest)


def block_levels(key, extent, cuts, least, high):
    gain, own = 1.0, jax.random.fold_in(key, 6)
    for position, parts in cuts:
        steps = jnp.exp(jax.random.uniform(jax.random.fold_in(own, position), (parts,), jnp.float32, least / len(cuts), high / len(cuts)))
        gain = gain * jnp.repeat(steps, extent[position] // parts).reshape([-1 if axis == position else 1 for axis in range(len(extent))])
    return gain


def bell_draw(key, dims, scale, limit, cuts=(), kind=jnp.bfloat16):
    array = scale * jax.random.normal(key, dims, jnp.float32)
    if cuts:
        array = array * block_levels(key, dims, cuts, -0.22, 0.18)
    return jnp.clip(array, -limit, limit).astype(kind)


def setup_inputs(seed: int = 0) -> dict:
    arg_keys = jax.random.split(jax.random.key(seed), 12)
    return {
        "positions": bell_draw(arg_keys[0], (3, ATOM_TOTAL), 1.2, 6.0, ((1, 512),), jnp.float32),
        "block_prev": bell_draw(arg_keys[1], (VECTORS, 3, ATOM_TOTAL), 1.0, 6.0, ((2, 512),), jnp.float32),
        "block_cur": bell_draw(arg_keys[2], (VECTORS, 3, ATOM_TOTAL), 1.0, 6.0, ((2, 512),), jnp.float32),
        "neighbours": set_ends(jax.random.randint(arg_keys[3], (SLOT_COUNT, ATOM_TOTAL), 0, EXTENDED), jax.random.fold_in(arg_keys[3], 1), 0, EXTENDED - 1).astype(jnp.int32),
        "counts": set_ends(jax.random.randint(arg_keys[4], (ATOM_TOTAL,), 1, SLOT_COUNT + 1), jax.random.fold_in(arg_keys[4], 1), 1, SLOT_COUNT).astype(jnp.int32),
        "x_lists": draw_x_lists(jax.random.fold_in(arg_keys[11], 71), 0),
        "y_lists": draw_y_lists(jax.random.fold_in(arg_keys[11], 71), 0),
        "w_radial": bell_draw(arg_keys[7], (BASIS_SIZE, CHANNELS), (BASIS_SIZE * SLOT_COUNT) ** -0.5, 0.375, (), jnp.float32),
        "w_vector": bell_draw(arg_keys[8], (BASIS_SIZE, CHANNELS), (2 * BASIS_SIZE) ** -0.5, 1.5, (), jnp.float32),
        "w_mix": bell_draw(arg_keys[9], (CHANNELS, CHANNELS), CHANNELS ** -0.5, 0.5, (), jnp.float32),
        "w_out": bell_draw(arg_keys[10], (CHANNELS,), CHANNELS ** -0.5, 0.5, (), jnp.float32),
    }


EXACT_DOT = lax.Precision.HIGHEST
SOFTEN = 0.25
CUTOFF = 5.0
GAUSS_WIDTH = 2.0

def edge_terms(vector):
    squared = jnp.sum(vector * vector) + SOFTEN
    radius = jnp.sqrt(squared)
    heading = vector / radius
    envelope = jnp.maximum(1.0 - squared / (CUTOFF * CUTOFF), 0.0) ** 3
    centers = CUTOFF * (jnp.arange(BASIS_SIZE, dtype=jnp.float32) + 0.5) / BASIS_SIZE
    radial = jnp.exp(-GAUSS_WIDTH * (radius - centers) ** 2) * envelope
    return jnp.concatenate([radial, radial * heading[0], radial * heading[1], radial * heading[2]])

def weighted_terms(vector, coeffs):
    return jnp.sum(coeffs * edge_terms(vector))

def edge_jacobian(vector):
    columns = jax.vmap(lambda tangent: jax.jvp(edge_terms, (vector,), (tangent,))[1])(jnp.eye(3, dtype=vector.dtype))
    return columns.T

def edge_curvature(vector, coeffs):
    slope = jax.grad(weighted_terms)
    ignored, pullback = jax.vjp(lambda point: slope(point, coeffs), vector)
    return jax.vmap(lambda row: pullback(row)[0])(jnp.eye(3, dtype=vector.dtype))

def atom_energy(descriptor, weights):
    w_radial, w_vector, w_mix, w_out = weights
    scalar = jnp.einsum('ka,kc->ac', descriptor[0], w_radial, precision=EXACT_DOT)
    vector_part = jnp.einsum('dka,kc->dac', descriptor[1:], w_vector, precision=EXACT_DOT)
    mixed_in = scalar + lax.optimization_barrier(jnp.sum(vector_part * vector_part, axis=0))
    hidden = jax.nn.silu(jnp.dot(mixed_in, w_mix, precision=EXACT_DOT))
    return jnp.sum(jnp.dot(hidden, w_out, precision=EXACT_DOT))

def prepare(own_pos, ext_pos, neighbours, counts, weights):
    atom_count = own_pos.shape[1]
    slot_count = neighbours.shape[0]
    flat_index = neighbours.reshape(-1)
    deltas = jnp.take(ext_pos, flat_index, axis=1) - jnp.tile(own_pos, (1, slot_count))
    valid_mask = (jnp.arange(slot_count, dtype=jnp.int32)[:, None] < counts[None, :]).astype(jnp.float32).reshape(-1)
    features = jax.vmap(edge_terms, in_axes=1, out_axes=1)(deltas) * valid_mask
    descriptor = lax.optimization_barrier(jnp.sum(features.reshape(4, BASIS_SIZE, slot_count, atom_count), axis=2))
    energy_grad = jax.grad(atom_energy)
    coeffs, pullback = jax.vjp(lambda current: energy_grad(current, weights), descriptor)

    def linearized(tangent):
        return pullback(tangent)[0]
    jacobian = jax.vmap(edge_jacobian, in_axes=1, out_axes=2)(deltas) * valid_mask
    coeff_edges = jnp.tile(coeffs.reshape(4 * BASIS_SIZE, atom_count), (1, slot_count))
    curvature = jax.vmap(edge_curvature, in_axes=(1, 1), out_axes=2)(deltas, coeff_edges) * valid_mask
    return (jacobian, curvature, linearized, flat_index)

def apply_hessian(pieces, tangents, atom_count):
    jacobian, curvature, linearized, flat_index = pieces
    vectors = tangents.shape[0]
    slot_count = flat_index.shape[0] // atom_count
    own_tan = tangents[:, :, :atom_count]
    moved_by = jnp.take(tangents, flat_index, axis=2) - jnp.tile(own_tan, (1, 1, slot_count))
    moved_by = moved_by.reshape(vectors, 3, slot_count, atom_count)
    jac_edges = jacobian.reshape(4 * BASIS_SIZE, 3, slot_count, atom_count)
    curv_edges = curvature.reshape(3, 3, slot_count, atom_count)
    change = jnp.einsum('kcsa,tcsa->tka', jac_edges, moved_by, precision=EXACT_DOT)
    descr_change = change.reshape(vectors, 4, BASIS_SIZE, atom_count)
    coeff_change = jax.vmap(linearized)(descr_change).reshape(vectors, 4 * BASIS_SIZE, atom_count)
    edge_out = jnp.einsum('kcsa,tka->tcsa', jac_edges, coeff_change, precision=EXACT_DOT)
    edge_out = edge_out + jnp.einsum('cgsa,tgsa->tcsa', curv_edges, moved_by, precision=EXACT_DOT)
    result = jnp.zeros_like(tangents).at[:, :, flat_index].add(edge_out.reshape(vectors, 3, slot_count * atom_count))
    return result.at[:, :, :atom_count].add(-lax.optimization_barrier(jnp.sum(edge_out, axis=2)))

def take_rows(data, index):
    return jax.vmap(jax.vmap(lambda block, picks: jnp.take(block, picks, axis=-1)))(data, index)

def add_rows(data, index, extra):
    return jax.vmap(jax.vmap(lambda block, picks, added: block.at[..., picks].add(added)))(data, index, extra)

def extend_all(data, grid_x, grid_y):
    widened = jnp.concatenate([data, jnp.roll(take_rows(data, grid_x[:, :, 0]), 1, axis=0), jnp.roll(take_rows(data, grid_x[:, :, 1]), -1, axis=0)], axis=-1)
    return jnp.concatenate([widened, jnp.roll(take_rows(widened, grid_y[:, :, 0]), 1, axis=1), jnp.roll(take_rows(widened, grid_y[:, :, 1]), -1, axis=1)], axis=-1)

def fold_all(result, grid_x, grid_y, atom_count, halo_rows):
    widened = atom_count + 2 * halo_rows
    buffer = result[..., :widened]
    buffer = add_rows(buffer, grid_y[:, :, 0], jnp.roll(result[..., widened:widened + halo_rows], -1, axis=1))
    buffer = add_rows(buffer, grid_y[:, :, 1], jnp.roll(result[..., widened + halo_rows:], 1, axis=1))
    own_rows = buffer[..., :atom_count]
    own_rows = add_rows(own_rows, grid_x[:, :, 0], jnp.roll(buffer[..., atom_count:atom_count + halo_rows], -1, axis=0))
    own_rows = add_rows(own_rows, grid_x[:, :, 1], jnp.roll(buffer[..., atom_count + halo_rows:widened], 1, axis=0))
    return own_rows

def orthonormal(work_block, newer_block, older_block, total_rows):
    vectors = work_block.shape[0]
    work_flat = work_block.reshape(vectors, -1)
    basis_rows = jnp.concatenate([newer_block.reshape(vectors, -1), older_block.reshape(vectors, -1)], 0)
    projection = jnp.dot(basis_rows, work_flat.T, precision=EXACT_DOT) / total_rows
    residual = work_flat - jnp.dot(projection.T, basis_rows, precision=EXACT_DOT)
    gram_matrix = jnp.dot(residual, residual.T, precision=EXACT_DOT) / total_rows
    lower_factor = jnp.linalg.cholesky(gram_matrix)
    fresh_block = lax.linalg.triangular_solve(lower_factor, residual, left_side=True, lower=True)
    return (fresh_block.reshape(work_block.shape), lower_factor)

def reference(positions, block_prev, block_cur, neighbours, counts, x_lists, y_lists, w_radial, w_vector, w_mix, w_out):
    weights = (w_radial, w_vector, w_mix, w_out)
    grid_x = x_lists.reshape(N_GX, N_GY, 2, HALO_ATOMS)
    grid_y = y_lists.reshape(N_GX, N_GY, 2, HALO_ATOMS)
    pos_grid = positions.reshape(3, N_GX, N_GY, ATOMS_DEV).transpose(1, 2, 0, 3)
    slot_grid = neighbours.reshape(SLOT_COUNT, N_GX, N_GY, ATOMS_DEV).transpose(1, 2, 0, 3).reshape(DOMAINS, SLOT_COUNT, ATOMS_DEV)
    count_grid = counts.reshape(DOMAINS, ATOMS_DEV)
    ext_pos = extend_all(pos_grid, grid_x, grid_y).reshape(DOMAINS, 3, EXTENDED)
    own_pos = pos_grid.reshape(DOMAINS, 3, ATOMS_DEV)

    def one_domain(domain_data):
        own_here, ext_here, tan_here, slots_here, counts_here = domain_data
        pieces = prepare(own_here, ext_here, slots_here, counts_here, weights)
        return apply_hessian(pieces, tan_here, ATOMS_DEV)

    def hessian_of(block):
        block_grid = block.reshape(VECTORS, 3, N_GX, N_GY, ATOMS_DEV).transpose(2, 3, 0, 1, 4)
        ext_tan = extend_all(block_grid, grid_x, grid_y).reshape(DOMAINS, VECTORS, 3, EXTENDED)
        result = lax.map(one_domain, (own_pos, ext_pos, ext_tan, slot_grid, count_grid))
        result = result.reshape(N_GX, N_GY, VECTORS, 3, EXTENDED)
        own_rows = fold_all(result, grid_x, grid_y, ATOMS_DEV, HALO_ATOMS)
        return own_rows.transpose(2, 3, 0, 1, 4).reshape(VECTORS, 3, ATOM_TOTAL)
    total_rows = 3.0 * ATOM_TOTAL
    older_block = block_prev
    newer_block = block_cur
    fresh_list = []
    factor_list = []
    for lanczos_step in range(LANCZOS_STEPS):
        work_block = hessian_of(newer_block)
        fresh_block, lower_factor = orthonormal(work_block, newer_block, older_block, total_rows)
        fresh_list.append(fresh_block)
        factor_list.append(lower_factor)
        older_block = newer_block
        newer_block = fresh_block
    return (jnp.stack(fresh_list), jnp.stack(factor_list))
```

```python
import functools

import jax
import jax.numpy as jnp
from jax import lax
from jax.experimental import pallas as pl
from jax.experimental.pallas import tpu as pltpu
from jax.sharding import PartitionSpec as P

MESH = pl.DeviceIdType.MESH
F32 = jnp.float32
BF16 = jnp.bfloat16
HIGHEST = lax.Precision.HIGHEST

VECTORS = 32
SLOTS = 32
ATOMS = 64
EXTENDED = 320
RAW = 576
SOFTEN = 0.25
CUTOFF = 5.0
BASIS_SIZE = 8
GROUPS = SLOTS // 4
HALF_GROUPS = 2 * GROUPS
META = 48

EX_NEWER, EX_OLDER, EX_FOLD_W, EX_WORK, EX_FOLD_Q, EX_FOLD_Y = range(6)


def split2(x):
    high = x.astype(BF16)
    low = (x - high.astype(F32)).astype(BF16)
    return high, low


def mm(a, b):
    return jnp.dot(a, b, preferred_element_type=F32)


def mm_t(a, b):
    return lax.dot_general(a, b, (((1,), (1,)), ((), ())), preferred_element_type=F32)


def dot3(a, b):
    a_high, a_low = split2(a)
    b_high, b_low = split2(b)
    return mm(a_high, b_high) + (mm(a_high, b_low) + mm(a_low, b_high))


def dot3_t(a, b):
    a_high, a_low = split2(a)
    b_high, b_low = split2(b)
    return mm_t(a_high, b_high) + (mm_t(a_high, b_low) + mm_t(a_low, b_high))


def exact(a, b):
    return jnp.dot(a, b, precision=HIGHEST, preferred_element_type=F32)


def exact_t(a, b):
    return lax.dot_general(a, b, (((1,), (1,)), ((), ())), precision=HIGHEST, preferred_element_type=F32)


def iota(shape, axis):
    return lax.broadcasted_iota(jnp.int32, shape, axis)


def factor_and_inverse(gram):
    n = gram.shape[0]
    row, column = iota((n, n), 0), iota((n, n), 1)
    wide_row = iota((n, 2 * n), 0)
    state = jnp.concatenate([gram, (row == column).astype(F32)], axis=1)
    lower = jnp.zeros((n, n), F32)
    for j in range(n):
        scale = lax.rsqrt(state[j : j + 1, j : j + 1])
        pivot_row = state[j : j + 1, :] * scale
        pivot_column = state[:, j : j + 1] * scale
        lower = jnp.where((column == j) & (row >= j), pivot_column, lower)
        state = jnp.where(wide_row > j, state - pivot_column * pivot_row, jnp.where(wide_row == j, pivot_row, state))
    return lower, state[:, n:]


def kernel(
    n_gx,
    n_gy,
    total_rows,
    pos_ref,
    prev_ref,
    cur_ref,
    nb_ref,
    cnt_ref,
    xl_ref,
    yl_ref,
    wr_ref,
    wv_ref,
    wmix_ref,
    wout_ref,
    out_ref,
    fac_ref,
    recv_n,
    recv_p,
    recv_w,
    fold_send,
    fold_recv,
    d_ref,
    sel_ref,
    fe_ref,
    ms_ref,
    mv_ref,
    dd_ref,
    cf_ref,
    g_ref,
    z_ref,
    pay_ref,
    rs_ref,
    zs_ref,
    tot_ref,
    ex_send,
    ex_recv,
    ar_send,
    ar_recv,
):
    n_z = n_gx // 2
    plane = 2 * n_gy
    rpd = 32 // plane
    gx = lax.axis_index("gx")
    gy = lax.axis_index("gy")
    z_pos, core = gx // 2, gx % 2
    me = gy * 2 + core

    def near(i):
        dp, dq = i // 3 - 1, i % 3 - 1
        return (gx + dp + n_gx) % n_gx, (gy + dq + n_gy) % n_gy

    def in_plane(r):
        return z_pos * 2 + r % 2, r // 2

    def off_own(j):
        return j + jnp.where(j >= 4, 1, 0)

    barrier = pltpu.get_barrier_semaphore()

    def greet_near(j, c):
        pl.semaphore_signal(barrier, inc=1, device_id=near(off_own(j)), device_id_type=MESH)
        return c

    def greet_plane(j, c):
        pl.semaphore_signal(barrier, inc=1, device_id=in_plane((me + j) % plane), device_id_type=MESH)
        return c

    def greet_line(j, c):
        pl.semaphore_signal(barrier, inc=1, device_id=(((z_pos + j) % n_z) * 2 + core, gy), device_id_type=MESH)
        return c

    lax.fori_loop(0, 8, greet_near, 0)
    lax.fori_loop(1, n_z, greet_line, 0)
    lax.fori_loop(1, plane, greet_plane, 0)

    def pack_own(source, target):
        for c in range(3):
            block = source[c]
            target[4, c * 16 : (c + 1) * 16, :] = jnp.concatenate([block[:16], block[16:]], axis=1)

    pack_own(cur_ref, recv_n)
    pack_own(prev_ref, recv_p)
    left = jnp.concatenate([pos_ref[...], jnp.zeros((5, ATOMS), F32)], axis=0)
    right = jnp.concatenate(
        [xl_ref[0].astype(F32), yl_ref[0].astype(F32), jnp.zeros((4, ATOMS), F32)], axis=0
    )
    recv_n[4, META : META + 8, :] = jnp.concatenate([left, right], axis=1)

    count_row = cnt_ref[...]
    count_row = jnp.concatenate([count_row] * 4, axis=1)
    lane = iota((1, 256), 1)

    def build_incidence(g, c):
        rows = [nb_ref[pl.ds(4 * g + s, 1), :] for s in range(4)]
        index = jnp.concatenate(rows, axis=1)
        valid = (4 * g + lane // ATOMS) < count_row
        index = jnp.where(valid, index, -1)
        own = jnp.where(valid, lane % ATOMS, -1)
        picked = (iota((EXTENDED, 256), 0) == index).astype(F32)
        minus = (iota((ATOMS, 256), 0) == own).astype(F32)
        d_ref[g] = jnp.concatenate([picked[:ATOMS] - minus, picked[ATOMS:]], axis=0).astype(BF16)
        return c

    lax.fori_loop(0, GROUPS, build_incidence, 0)

    w_vec = wv_ref[...]
    w_rad = wr_ref[...]
    w_mix = wmix_ref[...]
    w_mix_t = jnp.transpose(w_mix)
    pad = jnp.zeros((112, 128), F32)
    w_both_t = jnp.transpose(jnp.concatenate([w_rad, w_vec, pad], axis=0))
    w_rad_t = w_both_t[:, :8]
    w_vec_t = w_both_t[:, 8:16]
    w_out_t = jnp.transpose(jnp.broadcast_to(wout_ref[...], (128, 128)))
    level = jnp.sqrt(jnp.sum(wout_ref[...] * wout_ref[...])) * jnp.sqrt(jnp.sum(w_mix * w_mix)) * jnp.sum(w_vec * w_vec)
    shrink = 1.0 / jnp.clip(level, 1e-8, 1e8)
    grow = jnp.clip(level, 1e-8, 1e8)

    pl.semaphore_wait(barrier, 8 + (n_z - 1) + (plane - 1))

    def spread_copy(number, ref, i):
        return pltpu.make_async_remote_copy(
            src_ref=ref.at[4],
            dst_ref=ref.at[8 - i],
            send_sem=ex_send.at[number, i],
            recv_sem=ex_recv.at[number, 8 - i],
            device_id=near(i),
            device_id_type=MESH,
        )

    def fold_copy(number, slot, i):
        return pltpu.make_async_remote_copy(
            src_ref=fold_send.at[slot, i],
            dst_ref=fold_recv.at[slot, 8 - i],
            send_sem=ex_send.at[number, i],
            recv_sem=ex_recv.at[number, 8 - i],
            device_id=near(i),
            device_id_type=MESH,
        )

    def start_all(make):
        def one(j, c):
            make(off_own(j)).start()
            return c

        lax.fori_loop(0, 8, one, 0)

    def wait_all(make):
        def one(j, c):
            make(off_own(j)).wait()
            return c

        lax.fori_loop(0, 8, one, 0)

    newer = functools.partial(spread_copy, EX_NEWER, recv_n)
    older = functools.partial(spread_copy, EX_OLDER, recv_p)
    work = functools.partial(spread_copy, EX_WORK, recv_w)
    fold_w = functools.partial(fold_copy, EX_FOLD_W, 0)
    fold_q = functools.partial(fold_copy, EX_FOLD_Q, 1)
    fold_y = functools.partial(fold_copy, EX_FOLD_Y, 2)
    start_all(newer)
    start_all(older)

    def raw_rows(ref):
        pieces = []
        for c in range(3):
            for h in range(2):
                pieces.append(
                    jnp.concatenate(
                        [ref[i, c * 16 : (c + 1) * 16, h * ATOMS : (h + 1) * ATOMS] for i in range(9)], axis=1
                    )
                )
        return jnp.concatenate(pieces, axis=0)

    def extend(ref):
        high, low = split2(raw_rows(ref))
        return mm(jnp.concatenate([high, low], axis=0), sel_ref[...]).astype(BF16)

    wait_all(newer)

    def listed(slot, row):
        return recv_n[slot, META + row : META + row + 1, ATOMS:]

    own_row = iota((1, ATOMS), 1).astype(F32)

    def widened(own_slot, left_slot, right_slot):
        return jnp.concatenate(
            [own_row + own_slot * 64.0, listed(left_slot, 0) + left_slot * 64.0, listed(right_slot, 1) + right_slot * 64.0],
            axis=1,
        )

    def looked_up(table, picks):
        hot = (iota((3 * ATOMS, ATOMS), 0).astype(F32) == picks).astype(F32)
        return exact(jnp.broadcast_to(table, (8, 3 * ATOMS)), hot)[0:1]

    before = looked_up(widened(3, 0, 6), listed(3, 2))
    after = looked_up(widened(5, 2, 8), listed(5, 3))
    to_raw = jnp.concatenate([widened(4, 1, 7), before, after], axis=1)
    to_raw = (to_raw + 0.5).astype(jnp.int32)
    sel_ref[...] = (iota((RAW, EXTENDED), 0) == to_raw).astype(F32).astype(BF16)

    newer_ext = extend(recv_n)
    raw_pos = jnp.concatenate([recv_n[i, META : META + 8, :ATOMS] for i in range(9)], axis=1)
    p_high = raw_pos.astype(BF16)
    rest = raw_pos - p_high.astype(F32)
    p_mid = rest.astype(BF16)
    p_low = (rest - p_mid.astype(F32)).astype(BF16)
    zero8 = jnp.zeros((8, RAW), BF16)
    pos_ext = mm(jnp.concatenate([p_high, p_mid, p_low, zero8], axis=0), sel_ref[...]).astype(BF16)

    center = CUTOFF * (iota((BASIS_SIZE, 1), 0).astype(F32) + 0.5) / BASIS_SIZE
    descriptor = [jnp.zeros((BASIS_SIZE, 256), F32) for _ in range(4)]

    def edge_rows(g):
        parts = mm(pos_ext, d_ref[g])
        d = parts[0:8] + (parts[8:16] + parts[16:24])
        d = d[0:3]
        squared = jnp.sum(d * d, axis=0, keepdims=True) + SOFTEN
        inv_r = lax.rsqrt(squared)
        r = squared * inv_r
        h = d * inv_r
        q = jnp.maximum(1.0 - squared * (1.0 / (CUTOFF * CUTOFF)), 0.0)
        env = q * q * q
        env1 = (-6.0 / 25.0) * r * q * q
        env2 = (-6.0 / 25.0) * q * q + (24.0 / 625.0) * squared * q
        offset = r - center
        bell = jnp.exp(-2.0 * offset * offset)
        f = bell * env
        f1 = bell * (env1 - 4.0 * offset * env)
        f2 = bell * (env2 - 8.0 * offset * env1 + (16.0 * offset * offset - 4.0) * env)
        return d, h, inv_r, f, f1, f2

    def first_pass(g, descriptor):
        d, h, inv_r, f, f1, f2 = edge_rows(g)
        valid = ((4 * g + lane // ATOMS) < count_row).astype(F32)
        e = f1 - f * inv_r
        for half in range(2):
            cut = slice(half * 128, (half + 1) * 128)
            fe_ref[2 * g + half, 0:8, :] = f[:, cut]
            fe_ref[2 * g + half, 8:16, :] = f1[:, cut]
            fe_ref[2 * g + half, 16:24, :] = e[:, cut]
            ms_ref[2 * g + half, 0:3, :] = h[:, cut]
            ms_ref[2 * g + half, 3:4, :] = inv_r[:, cut]
            fe_ref[2 * g + half, 24:32, :] = f2[:, cut]
        masked = f * valid
        return (
            descriptor[0] + masked,
            descriptor[1] + masked * h[0:1],
            descriptor[2] + masked * h[1:2],
            descriptor[3] + masked * h[2:3],
        )

    descriptor = lax.fori_loop(0, GROUPS, first_pass, tuple(descriptor))

    def fold_lanes(x):
        x = x[:, :128] + x[:, 128:]
        return x + pltpu.roll(x, 64, 1)

    descriptor = [fold_lanes(x) for x in descriptor]

    v = [exact(w_vec_t, descriptor[c + 1]) for c in range(3)]
    mixed_in = exact(w_rad_t, descriptor[0]) + (v[0] * v[0] + v[1] * v[1] + v[2] * v[2])
    x = exact(w_mix_t, mixed_in)
    gate = jax.nn.sigmoid(x)
    slope = gate * (1.0 - gate)
    silu1 = gate + x * slope
    silu2 = slope * (2.0 + x * (1.0 - 2.0 * gate))
    grad_m = exact(w_mix, w_out_t * silu1)
    bend = w_out_t * silu2
    coeffs = [exact(w_rad, grad_m)] + [exact(w_vec, 2.0 * v[c] * grad_m) for c in range(3)]

    low_lane = iota((1, 128), 1) < 64
    w_rad_hl = split2(w_rad)
    w_vec_hl = split2(w_vec)
    mix_hl = split2(w_mix)
    mix_t_hl = split2(w_mix_t)

    def dot_pre(a, b):
        b_high, b_low = split2(b)
        return mm(a[0], b_high) + (mm(a[0], b_low) + mm(a[1], b_high))

    for kind in range(4):
        table = w_rad_t if kind == 0 else w_vec_t
        columns = [jnp.where(low_lane, table[:, 2 * m : 2 * m + 1], table[:, 2 * m + 1 : 2 * m + 2]) for m in range(4)]
        base = columns if kind == 0 else [2.0 * v[kind - 1] * column for column in columns]
        moved = jnp.concatenate(base, axis=1)
        bend4 = jnp.concatenate([bend] * 4, axis=1)
        shift = dot_pre(mix_hl, bend4 * dot_pre(mix_t_hl, moved))
        parts = [dot_pre(w_rad_hl, shift)]
        for c in range(3):
            term = jnp.concatenate([2.0 * v[c]] * 4, axis=1) * shift
            if kind == c + 1:
                term = term + jnp.concatenate([2.0 * grad_m * column for column in columns], axis=1)
            parts.append(dot_pre(w_vec_hl, term))
        block = jnp.concatenate(parts, axis=0)
        for m in range(4):
            piece = block[:, m * 128 : (m + 1) * 128]
            turned = pltpu.roll(piece, 64, 1)
            g_ref[kind * 8 + 2 * m] = jnp.where(low_lane, piece, turned)
            g_ref[kind * 8 + 2 * m + 1] = jnp.where(low_lane, turned, piece)

    def second_pass(hg, c):
        f, f1, f2 = fe_ref[hg, 0:8, :], fe_ref[hg, 8:16, :], fe_ref[hg, 24:32, :]
        h = [ms_ref[hg, b : b + 1, :] for b in range(3)]
        inv_r = ms_ref[hg, 3:4, :]
        r = 1.0 / inv_r

        def total(coeff, values):
            return jnp.sum(coeff * values, axis=0, keepdims=True)

        s2 = total(coeffs[0], f2)
        s1 = total(coeffs[0], f1)
        for b in range(3):
            psi, psi1, psi2 = (total(coeffs[b + 1], values) for values in (f, f1, f2))
            chi1 = (psi1 - psi * inv_r) * inv_r
            chi2 = (psi2 - 2.0 * chi1) * inv_r
            d_b = h[b] * r
            s2 = s2 + d_b * chi2
            s1 = s1 + d_b * chi1
            ms_ref[hg, 6 + b : 7 + b, :] = chi1
        s1 = s1 * inv_r
        ms_ref[hg, 4:5, :] = s2 - s1
        ms_ref[hg, 5:6, :] = s1
        return c

    lax.fori_loop(0, HALF_GROUPS, second_pass, 0)

    def wide(row):
        return jnp.broadcast_to(row, (8, 128))

    def change_of(ext):
        def gather(g, c):
            moved = mm(ext, d_ref[g])
            moved = moved[:96] + moved[96:]
            mv_ref[2 * g] = moved[:, :128].reshape(3, 4, 8, 128)
            mv_ref[2 * g + 1] = moved[:, 128:].reshape(3, 4, 8, 128)
            return c

        lax.fori_loop(0, GROUPS, gather, 0)

        def tile(tt, c):
            def edges(hg, acc):
                u = [mv_ref[hg, b, tt] for b in range(3)]
                h = [wide(ms_ref[hg, b : b + 1, :]) for b in range(3)]
                inv_r = wide(ms_ref[hg, 3:4, :])
                rho = h[0] * u[0] + h[1] * u[1] + h[2] * u[2]
                scaled = [u[b] * inv_r for b in range(3)]
                along = [h[b] * rho for b in range(3)]
                new = list(acc)
                for k in range(8):
                    f = wide(fe_ref[hg, k : k + 1, :])
                    f1 = wide(fe_ref[hg, 8 + k : 9 + k, :])
                    e = wide(fe_ref[hg, 16 + k : 17 + k, :])
                    new[k] = acc[k] + f1 * rho
                    for b in range(3):
                        at = 8 * (b + 1) + k
                        new[at] = acc[at] + (f * scaled[b] + e * along[b])
                return tuple(new)

            acc = lax.fori_loop(0, HALF_GROUPS, edges, tuple(jnp.zeros((8, 128), F32) for _ in range(32)))
            for j in range(32):
                dd_ref[tt, j] = acc[j] + pltpu.roll(acc[j], 64, 1)
            return c

        lax.fori_loop(0, 4, tile, 0)

    def response():
        def pair(p, c):
            def one(j, acc):
                delta = jnp.where(low_lane, dd_ref[2 * p, j], dd_ref[2 * p + 1, j])
                return tuple(acc[i] + wide(g_ref[j, i : i + 1, :]) * delta for i in range(32))

            acc = lax.fori_loop(0, 32, one, tuple(jnp.zeros((8, 128), F32) for _ in range(32)))
            for i in range(32):
                turned = pltpu.roll(acc[i], 64, 1)
                cf_ref[2 * p, i] = jnp.where(low_lane, acc[i], turned)
                cf_ref[2 * p + 1, i] = jnp.where(low_lane, turned, acc[i])
            return c

        lax.fori_loop(0, 2, pair, 0)

    def forces(slot):
        def tile(tt, c):
            a = [cf_ref[tt, i] for i in range(32)]

            def edges(hg, c2):
                u = [mv_ref[hg, b, tt] for b in range(3)]
                h = [wide(ms_ref[hg, b : b + 1, :]) for b in range(3)]
                inv_r = wide(ms_ref[hg, 3:4, :])
                alpha = wide(ms_ref[hg, 4:5, :])
                beta = wide(ms_ref[hg, 5:6, :])
                chi = [wide(ms_ref[hg, 6 + b : 7 + b, :]) for b in range(3)]
                rho = h[0] * u[0] + h[1] * u[1] + h[2] * u[2]
                level = alpha * rho + (chi[0] * u[0] + chi[1] * u[1] + chi[2] * u[2])
                across = [None] * 3
                along = [None] * 3
                for k in range(8):
                    f = wide(fe_ref[hg, k : k + 1, :])
                    f1 = wide(fe_ref[hg, 8 + k : 9 + k, :])
                    e = wide(fe_ref[hg, 16 + k : 17 + k, :])
                    level = level + f1 * a[k]
                    for b in range(3):
                        coeff = a[8 * (b + 1) + k]
                        across[b] = f * coeff if k == 0 else across[b] + f * coeff
                        along[b] = e * coeff if k == 0 else along[b] + e * coeff
                level = level + (h[0] * along[0] + h[1] * along[1] + h[2] * along[2])
                for b in range(3):
                    mv_ref[hg, b, tt] = inv_r * across[b] + beta * u[b] + h[b] * level + chi[b] * rho
                return c2

            lax.fori_loop(0, HALF_GROUPS, edges, 0)
            return c

        lax.fori_loop(0, 4, tile, 0)

        def scatter(g, acc):
            edge = jnp.concatenate([mv_ref[2 * g].reshape(96, 128), mv_ref[2 * g + 1].reshape(96, 128)], axis=1)
            high, low = split2(edge)
            return acc + mm_t(jnp.concatenate([high, low], axis=0), d_ref[g])

        both = lax.fori_loop(0, GROUPS, scatter, jnp.zeros((192, EXTENDED), F32))
        high, low = split2(both[:96] + both[96:])
        raw = mm_t(jnp.concatenate([high, low], axis=0), sel_ref[...])
        raw = raw[:96] + raw[96:]
        for i in range(9):
            part = raw[:, i * ATOMS : (i + 1) * ATOMS]
            for c in range(3):
                top, bottom = part[c * 32 : c * 32 + 16], part[c * 32 + 16 : c * 32 + 32]
                fold_send[slot, i, c * 16 : (c + 1) * 16, :] = jnp.concatenate([top, bottom], axis=1)

    def folded(slot):
        total = fold_send[slot, 4]
        for i in range(9):
            if i != 4:
                total = total + fold_recv[slot, i]
        return total

    def keep_rows(at, packed):
        for h in range(2):
            z_ref[at + h * 16 : at + h * 16 + 16, :] = jnp.concatenate(
                [packed[c * 16 : (c + 1) * 16, h * ATOMS : (h + 1) * ATOMS] for c in range(3)], axis=1
            )

    change_of(newer_ext)
    response()
    forces(0)
    start_all(fold_w)

    wait_all(older)
    change_of(extend(recv_p))
    keep_rows(96, recv_n[4, 0:48, :])
    keep_rows(128, recv_p[4])

    wait_all(fold_w)
    recv_w[4] = folded(0)
    start_all(work)

    response()
    forces(1)
    start_all(fold_q)
    keep_rows(32, recv_w[4])

    wait_all(work)
    change_of(extend(recv_w))
    response()
    forces(2)
    start_all(fold_y)

    wait_all(fold_q)
    keep_rows(64, folded(1))
    wait_all(fold_y)
    keep_rows(0, folded(2) * shrink)

    y_rows, w_rows, q_rows = z_ref[0:32, :], z_ref[32:64, :], z_ref[64:96, :]
    n_rows, p_rows = z_ref[96:128, :], z_ref[128:160, :]
    none = jnp.zeros((32, 192), F32)
    pay_ref[:, 0, :] = dot3_t(w_rows, jnp.concatenate([w_rows, n_rows, p_rows, q_rows], axis=0))
    pay_ref[:, 1, :] = dot3_t(y_rows, jnp.concatenate([y_rows, w_rows, q_rows, none], axis=0))
    pay_ref[:, 2, :] = dot3_t(p_rows, jnp.concatenate([p_rows, n_rows, q_rows, none], axis=0))
    pay_ref[:, 3, :] = dot3_t(n_rows, jnp.concatenate([n_rows, none, none, none], axis=0)) + dot3_t(
        q_rows, jnp.concatenate([none, q_rows, none, none], axis=0)
    )

    def slice_of(ref, r):
        return ref.at[pl.ds(r * rpd, rpd)]

    def stage0(j):
        peer = (me + j) % plane
        return pltpu.make_async_remote_copy(
            src_ref=slice_of(pay_ref, peer),
            dst_ref=rs_ref.at[me],
            send_sem=ar_send.at[0, j],
            recv_sem=ar_recv.at[0, j],
            device_id=in_plane(peer),
            device_id_type=MESH,
        )

    def stage1(j):
        return pltpu.make_async_remote_copy(
            src_ref=zs_ref.at[z_pos],
            dst_ref=zs_ref.at[z_pos],
            send_sem=ar_send.at[1, j],
            recv_sem=ar_recv.at[1, j],
            device_id=(((z_pos + j) % n_z) * 2 + core, gy),
            device_id_type=MESH,
        )

    def stage2(j):
        return pltpu.make_async_remote_copy(
            src_ref=slice_of(tot_ref, me),
            dst_ref=slice_of(tot_ref, me),
            send_sem=ar_send.at[2, j],
            recv_sem=ar_recv.at[2, j],
            device_id=in_plane((me + j) % plane),
            device_id_type=MESH,
        )

    def run(make, count):
        def begin(j, c):
            make(j).start()
            return c

        def end(j, c):
            make(j).wait()
            return c

        lax.fori_loop(1, count, begin, 0)
        lax.fori_loop(1, count, end, 0)

    rs_ref[me] = pay_ref[pl.ds(me * rpd, rpd)]
    run(stage0, plane)
    zs_ref[z_pos] = jnp.sum(rs_ref[...], axis=0)
    run(stage1, n_z)
    tot_ref[pl.ds(me * rpd, rpd)] = jnp.sum(zs_ref[...], axis=0) * (1.0 / total_rows)
    run(stage2, plane)

    g1, g2, g3, g4 = (tot_ref[:, j, :] for j in range(4))
    t1, t2, t3 = (jnp.transpose(g) for g in (g1, g2, g3))

    def block(source, i):
        return source[:, i * 32 : (i + 1) * 32]

    def tblock(source, i):
        return source[i * 32 : (i + 1) * 32]

    ww, wn, wp, wq = (block(g1, i) for i in range(4))
    wq_s, ww_s, qw = wq * shrink, ww * shrink, tblock(t1, 3)
    column_y = jnp.concatenate([block(g2, 0), tblock(t2, 1), tblock(t2, 2), ww_s, qw * shrink], axis=0)
    column_w = jnp.concatenate([block(g2, 1), ww, qw, tblock(t1, 1), tblock(t1, 2)], axis=0)
    column_q = jnp.concatenate([block(g2, 2), wq, block(g4, 1), wp, block(g3, 2)], axis=0)
    column_n = jnp.concatenate([ww_s, wn, tblock(t1, 2), block(g4, 0), block(g3, 1)], axis=0)
    column_p = jnp.concatenate([wq_s, wp, tblock(t3, 2), tblock(t3, 1), block(g3, 0)], axis=0)
    gram = jnp.concatenate([column_y, column_w, column_q, column_n, column_p], axis=1)

    eye = (iota((32, 32), 0) == iota((32, 32), 1)).astype(F32)
    zero = jnp.zeros((32, 32), F32)
    resid1 = jnp.concatenate([zero, eye, zero, -wn, -wp], axis=1)
    image1 = jnp.concatenate([eye * grow, -wn, -wp, zero, zero], axis=1)
    lower1, inverse1 = factor_and_inverse(exact_t(exact(resid1, gram), resid1))
    fresh1 = exact(inverse1, resid1)
    work2 = exact(inverse1, image1)
    product = exact(work2, gram)
    on_newer = iota((32, 160), 1) // 32 == 3
    resid2 = work2 - exact(exact_t(product, fresh1), fresh1) - jnp.where(on_newer, product, 0.0)
    lower2, inverse2 = factor_and_inverse(exact_t(exact(resid2, gram), resid2))
    fresh2 = exact(inverse2, resid2)
    fac_ref[0] = lower1
    fac_ref[1] = lower2
    fresh = dot3(jnp.concatenate([fresh1, fresh2], axis=0), z_ref[...])
    for s in range(2):
        for c in range(3):
            out_ref[s, c] = fresh[s * 32 : (s + 1) * 32, c * ATOMS : (c + 1) * ATOMS]


def shards(n_gx, n_gy, positions, block_prev, block_cur, neighbours, counts, x_lists, y_lists, w_radial, w_vector, w_mix, w_out):
    n_z, plane = n_gx // 2, 2 * n_gy
    rpd = 32 // plane
    total_rows = 3.0 * ATOMS * n_gx * n_gy
    vmem = pl.BlockSpec(memory_space=pltpu.VMEM)
    blocks, factors = pl.pallas_call(
        functools.partial(kernel, n_gx, n_gy, total_rows),
        out_shape=(
            jax.ShapeDtypeStruct((2, 3, VECTORS, ATOMS), F32),
            jax.ShapeDtypeStruct((2, VECTORS, VECTORS), F32),
        ),
        in_specs=[vmem] * 11,
        out_specs=(vmem, vmem),
        scratch_shapes=[
            pltpu.VMEM((9, META + 8, 128), F32),
            pltpu.VMEM((9, 48, 128), F32),
            pltpu.VMEM((9, 48, 128), F32),
            pltpu.VMEM((3, 9, 48, 128), F32),
            pltpu.VMEM((3, 9, 48, 128), F32),
            pltpu.VMEM((GROUPS, EXTENDED, 256), BF16),
            pltpu.VMEM((RAW, EXTENDED), BF16),
            pltpu.VMEM((HALF_GROUPS, 32, 128), F32),
            pltpu.VMEM((HALF_GROUPS, 16, 128), F32),
            pltpu.VMEM((HALF_GROUPS, 3, 4, 8, 128), F32),
            pltpu.VMEM((4, 32, 8, 128), F32),
            pltpu.VMEM((4, 32, 8, 128), F32),
            pltpu.VMEM((32, 32, 128), F32),
            pltpu.VMEM((160, 192), F32),
            pltpu.VMEM((32, 4, 128), F32),
            pltpu.VMEM((plane, rpd, 4, 128), F32),
            pltpu.VMEM((n_z, rpd, 4, 128), F32),
            pltpu.VMEM((32, 4, 128), F32),
            pltpu.SemaphoreType.DMA((6, 9)),
            pltpu.SemaphoreType.DMA((6, 9)),
            pltpu.SemaphoreType.DMA((3, 32)),
            pltpu.SemaphoreType.DMA((3, 32)),
        ],
        compiler_params=pltpu.CompilerParams(collective_id=0, has_side_effects=True),
    )(
        positions,
        jnp.transpose(block_prev, (1, 0, 2)),
        jnp.transpose(block_cur, (1, 0, 2)),
        neighbours,
        counts.reshape(1, ATOMS),
        x_lists,
        y_lists,
        w_radial,
        w_vector,
        w_mix,
        w_out.reshape(1, 128),
    )
    return jnp.transpose(blocks, (0, 2, 1, 3)), factors


def solution(mesh):
    placed = (
        P(None, ("gx", "gy")),
        P(None, None, ("gx", "gy")),
        P(None, None, ("gx", "gy")),
        P(None, ("gx", "gy")),
        P(("gx", "gy")),
        P(("gx", "gy"), None, None),
        P(("gx", "gy"), None, None),
        P(),
        P(),
        P(),
        P(),
    )
    return jax.shard_map(
        functools.partial(shards, mesh.shape["gx"], mesh.shape["gy"]),
        mesh=mesh,
        in_specs=placed,
        out_specs=(P(None, None, None, ("gx", "gy")), P()),
        check_vma=False,
    )
```

```python
import functools

import jax
import jax.numpy as jnp
from jax import lax
from jax.experimental import pallas as pl
from jax.experimental.pallas import tpu as pltpu
from jax.sharding import PartitionSpec as P

MESH = pl.DeviceIdType.MESH
F32 = jnp.float32
BF16 = jnp.bfloat16
HIGHEST = lax.Precision.HIGHEST

VECTORS = 32
SLOTS = 32
ATOMS = 64
EXTENDED = 320
RAW = 576
SOFTEN = 0.25
CUTOFF = 5.0
BASIS_SIZE = 8
GROUPS = SLOTS // 4
HALF_GROUPS = 2 * GROUPS
META = 48
PIVOTS = 4

EX_NEWER, EX_OLDER, EX_FOLD_W, EX_WORK, EX_FOLD_Q, EX_FOLD_Y = range(6)


def split2(x):
    high = x.astype(BF16)
    low = (x - high.astype(F32)).astype(BF16)
    return high, low


def mm(a, b):
    return jnp.dot(a, b, preferred_element_type=F32)


def mm_t(a, b):
    return lax.dot_general(a, b, (((1,), (1,)), ((), ())), preferred_element_type=F32)


def dot3(a, b):
    a_high, a_low = split2(a)
    b_high, b_low = split2(b)
    return mm(a_high, b_high) + (mm(a_high, b_low) + mm(a_low, b_high))


def dot3_t(a, b):
    a_high, a_low = split2(a)
    b_high, b_low = split2(b)
    return mm_t(a_high, b_high) + (mm_t(a_high, b_low) + mm_t(a_low, b_high))


def exact(a, b):
    return jnp.dot(a, b, precision=HIGHEST, preferred_element_type=F32)


def exact_t(a, b):
    return lax.dot_general(a, b, (((1,), (1,)), ((), ())), precision=HIGHEST, preferred_element_type=F32)


def iota(shape, axis):
    return lax.broadcasted_iota(jnp.int32, shape, axis)


def factor_and_inverse(gram):
    n = gram.shape[0]
    row, column = iota((n, n), 0), iota((n, n), 1)
    wide_row = iota((n, 2 * n), 0)
    state = jnp.concatenate([gram, (row == column).astype(F32)], axis=1)
    lower = jnp.zeros((n, n), F32)
    for j in range(0, n, PIVOTS):
        at = [slice(j + p, j + p + 1) for p in range(PIVOTS)]
        small, scale, rows, columns = [], [], [], []
        for p in range(PIVOTS):
            entries = []
            for q in range(p):
                entry = state[at[p], at[q]]
                for m in range(q):
                    entry = entry - entries[m] * small[q][m]
                entries.append(entry * scale[q])
            pivot = state[at[p], at[p]]
            for m in range(p):
                pivot = pivot - entries[m] * entries[m]
            small.append(entries)
            scale.append(lax.rsqrt(pivot))
        for p in range(PIVOTS):
            pivot_row, pivot_column = state[at[p], :], state[:, at[p]]
            for m in range(p):
                pivot_row = pivot_row - small[p][m] * rows[m]
                pivot_column = pivot_column - small[p][m] * columns[m]
            rows.append(pivot_row * scale[p])
            columns.append(pivot_column * scale[p])
        below = state
        for p in range(PIVOTS):
            below = below - columns[p] * rows[p]
            lower = jnp.where((column == j + p) & (row >= j + p), columns[p], lower)
        state = jnp.where(wide_row >= j + PIVOTS, below, state)
        for p in range(PIVOTS):
            state = jnp.where(wide_row == j + p, rows[p], state)
    return lower, state[:, n:]


def kernel(
    n_gx,
    n_gy,
    total_rows,
    pos_ref,
    prev_ref,
    cur_ref,
    nb_ref,
    cnt_ref,
    xl_ref,
    yl_ref,
    wr_ref,
    wv_ref,
    wmix_ref,
    wout_ref,
    out_ref,
    fac_ref,
    recv_n,
    recv_p,
    recv_w,
    fold_send,
    fold_recv,
    d_ref,
    sel_ref,
    fe_ref,
    ms_ref,
    mv_ref,
    dd_ref,
    cf_ref,
    g_ref,
    z_ref,
    pay_ref,
    rs_ref,
    zs_ref,
    tot_ref,
    ex_send,
    ex_recv,
    ar_send,
    ar_recv,
):
    n_z = n_gx // 2
    plane = 2 * n_gy
    rpd = 32 // plane
    gx = lax.axis_index("gx")
    gy = lax.axis_index("gy")
    z_pos, core = gx // 2, gx % 2
    me = gy * 2 + core

    def wrapped(value, size):
        return jnp.where(value >= size, value - size, value)

    gx_near = (wrapped(gx + (n_gx - 1), n_gx), gx, wrapped(gx + 1, n_gx))
    gy_near = (wrapped(gy + (n_gy - 1), n_gy), gy, wrapped(gy + 1, n_gy))
    others = [i for i in range(9) if i != 4]

    def near(i):
        return gx_near[i // 3], gy_near[i % 3]

    def plane_peer(dy, flip):
        to_y = wrapped(gy + dy, n_gy)
        to_core = 1 - core if flip else core
        return to_y * 2 + to_core, (z_pos * 2 + to_core, to_y)

    def line_peer(dz):
        return wrapped(z_pos + dz, n_z) * 2 + core, gy

    def each_plane(act):
        act(0, True)

        def body(dy, c):
            act(dy, False)
            act(dy, True)
            return c

        lax.fori_loop(1, n_gy, body, 0)

    def each_line(act):
        def body(dz, c):
            act(dz)
            return c

        lax.fori_loop(1, n_z, body, 0)

    barrier = pltpu.get_barrier_semaphore()

    def greet(device):
        pl.semaphore_signal(barrier, inc=1, device_id=device, device_id_type=MESH)

    for i in others:
        greet(near(i))
    each_line(lambda dz: greet(line_peer(dz)))
    each_plane(lambda dy, flip: greet(plane_peer(dy, flip)[1]))

    def pack_own(source, target):
        for c in range(3):
            block = source[c]
            target[4, c * 16 : (c + 1) * 16, :] = jnp.concatenate([block[:16], block[16:]], axis=1)

    pack_own(cur_ref, recv_n)
    pack_own(prev_ref, recv_p)
    left = jnp.concatenate([pos_ref[...], jnp.zeros((5, ATOMS), F32)], axis=0)
    right = jnp.concatenate(
        [xl_ref[0].astype(F32), yl_ref[0].astype(F32), jnp.zeros((4, ATOMS), F32)], axis=0
    )
    recv_n[4, META : META + 8, :] = jnp.concatenate([left, right], axis=1)

    pl.semaphore_wait(barrier, 8 + (n_z - 1) + (plane - 1))

    def spread_copy(number, ref, i):
        return pltpu.make_async_remote_copy(
            src_ref=ref.at[4],
            dst_ref=ref.at[8 - i],
            send_sem=ex_send.at[number, i],
            recv_sem=ex_recv.at[number, 8 - i],
            device_id=near(i),
            device_id_type=MESH,
        )

    def fold_copy(number, slot, i):
        return pltpu.make_async_remote_copy(
            src_ref=fold_send.at[slot, i],
            dst_ref=fold_recv.at[slot, 8 - i],
            send_sem=ex_send.at[number, i],
            recv_sem=ex_recv.at[number, 8 - i],
            device_id=near(i),
            device_id_type=MESH,
        )

    def start_all(make):
        for i in others:
            make(i).start()

    def wait_all(make):
        for i in others:
            make(i).wait()

    newer = functools.partial(spread_copy, EX_NEWER, recv_n)
    older = functools.partial(spread_copy, EX_OLDER, recv_p)
    work = functools.partial(spread_copy, EX_WORK, recv_w)
    fold_w = functools.partial(fold_copy, EX_FOLD_W, 0)
    fold_q = functools.partial(fold_copy, EX_FOLD_Q, 1)
    fold_y = functools.partial(fold_copy, EX_FOLD_Y, 2)
    start_all(newer)
    start_all(older)

    count_row = cnt_ref[...]
    count_row = jnp.concatenate([count_row] * 4, axis=1)
    lane = iota((1, 256), 1)

    def build_incidence(g, c):
        rows = [nb_ref[pl.ds(4 * g + s, 1), :] for s in range(4)]
        index = jnp.concatenate(rows, axis=1)
        valid = (4 * g + lane // ATOMS) < count_row
        index = jnp.where(valid, index, -1)
        own = jnp.where(valid, lane % ATOMS, -1)
        picked = (iota((EXTENDED, 256), 0) == index).astype(F32)
        minus = (iota((ATOMS, 256), 0) == own).astype(F32)
        d_ref[g] = jnp.concatenate([picked[:ATOMS] - minus, picked[ATOMS:]], axis=0).astype(BF16)
        return c

    lax.fori_loop(0, GROUPS, build_incidence, 0)

    w_vec = wv_ref[...]
    w_rad = wr_ref[...]
    w_mix = wmix_ref[...]
    w_mix_t = jnp.transpose(w_mix)
    pad = jnp.zeros((112, 128), F32)
    w_both_t = jnp.transpose(jnp.concatenate([w_rad, w_vec, pad], axis=0))
    w_rad_t = w_both_t[:, :8]
    w_vec_t = w_both_t[:, 8:16]
    w_out_t = jnp.transpose(jnp.broadcast_to(wout_ref[...], (128, 128)))
    level = jnp.sqrt(jnp.sum(wout_ref[...] * wout_ref[...])) * jnp.sqrt(jnp.sum(w_mix * w_mix)) * jnp.sum(w_vec * w_vec)
    shrink = 1.0 / jnp.clip(level, 1e-8, 1e8)
    grow = jnp.clip(level, 1e-8, 1e8)

    def raw_rows(ref):
        pieces = []
        for c in range(3):
            for h in range(2):
                pieces.append(
                    jnp.concatenate(
                        [ref[i, c * 16 : (c + 1) * 16, h * ATOMS : (h + 1) * ATOMS] for i in range(9)], axis=1
                    )
                )
        return jnp.concatenate(pieces, axis=0)

    def extend(ref):
        high, low = split2(raw_rows(ref))
        return mm(jnp.concatenate([high, low], axis=0), sel_ref[...]).astype(BF16)

    wait_all(newer)

    def listed(slot, row):
        return recv_n[slot, META + row : META + row + 1, ATOMS:]

    own_row = iota((1, ATOMS), 1).astype(F32)

    def widened(own_slot, left_slot, right_slot):
        return jnp.concatenate(
            [own_row + own_slot * 64.0, listed(left_slot, 0) + left_slot * 64.0, listed(right_slot, 1) + right_slot * 64.0],
            axis=1,
        )

    def looked_up(table, picks):
        hot = (iota((3 * ATOMS, ATOMS), 0).astype(F32) == picks).astype(F32)
        return exact(jnp.broadcast_to(table, (8, 3 * ATOMS)), hot)[0:1]

    before = looked_up(widened(3, 0, 6), listed(3, 2))
    after = looked_up(widened(5, 2, 8), listed(5, 3))
    to_raw = jnp.concatenate([widened(4, 1, 7), before, after], axis=1)
    to_raw = (to_raw + 0.5).astype(jnp.int32)
    sel_ref[...] = (iota((RAW, EXTENDED), 0) == to_raw).astype(F32).astype(BF16)

    newer_ext = extend(recv_n)
    raw_pos = jnp.concatenate([recv_n[i, META : META + 8, :ATOMS] for i in range(9)], axis=1)
    p_high = raw_pos.astype(BF16)
    rest = raw_pos - p_high.astype(F32)
    p_mid = rest.astype(BF16)
    p_low = (rest - p_mid.astype(F32)).astype(BF16)
    zero8 = jnp.zeros((8, RAW), BF16)
    pos_ext = mm(jnp.concatenate([p_high, p_mid, p_low, zero8], axis=0), sel_ref[...]).astype(BF16)

    center = CUTOFF * (iota((BASIS_SIZE, 1), 0).astype(F32) + 0.5) / BASIS_SIZE
    descriptor = [jnp.zeros((BASIS_SIZE, 256), F32) for _ in range(4)]

    def edge_rows(g):
        parts = mm(pos_ext, d_ref[g])
        d = parts[0:8] + (parts[8:16] + parts[16:24])
        d = d[0:3]
        squared = jnp.sum(d * d, axis=0, keepdims=True) + SOFTEN
        inv_r = lax.rsqrt(squared)
        r = squared * inv_r
        h = d * inv_r
        q = jnp.maximum(1.0 - squared * (1.0 / (CUTOFF * CUTOFF)), 0.0)
        env = q * q * q
        env1 = (-6.0 / 25.0) * r * q * q
        env2 = (-6.0 / 25.0) * q * q + (24.0 / 625.0) * squared * q
        offset = r - center
        bell = jnp.exp(-2.0 * offset * offset)
        f = bell * env
        f1 = bell * (env1 - 4.0 * offset * env)
        f2 = bell * (env2 - 8.0 * offset * env1 + (16.0 * offset * offset - 4.0) * env)
        return d, h, inv_r, f, f1, f2

    def first_pass(g, descriptor):
        d, h, inv_r, f, f1, f2 = edge_rows(g)
        valid = ((4 * g + lane // ATOMS) < count_row).astype(F32)
        e = f1 - f * inv_r
        for half in range(2):
            cut = slice(half * 128, (half + 1) * 128)
            fe_ref[2 * g + half, 0:8, :] = f[:, cut]
            fe_ref[2 * g + half, 8:16, :] = f1[:, cut]
            fe_ref[2 * g + half, 16:24, :] = e[:, cut]
            ms_ref[2 * g + half, 0:3, :] = h[:, cut]
            ms_ref[2 * g + half, 3:4, :] = inv_r[:, cut]
            fe_ref[2 * g + half, 24:32, :] = f2[:, cut]
        masked = f * valid
        return (
            descriptor[0] + masked,
            descriptor[1] + masked * h[0:1],
            descriptor[2] + masked * h[1:2],
            descriptor[3] + masked * h[2:3],
        )

    descriptor = lax.fori_loop(0, GROUPS, first_pass, tuple(descriptor), unroll=True)

    def fold_lanes(x):
        x = x[:, :128] + x[:, 128:]
        return x + pltpu.roll(x, 64, 1)

    descriptor = [fold_lanes(x) for x in descriptor]

    v = [exact(w_vec_t, descriptor[c + 1]) for c in range(3)]
    mixed_in = exact(w_rad_t, descriptor[0]) + (v[0] * v[0] + v[1] * v[1] + v[2] * v[2])
    x = exact(w_mix_t, mixed_in)
    gate = jax.nn.sigmoid(x)
    slope = gate * (1.0 - gate)
    silu1 = gate + x * slope
    silu2 = slope * (2.0 + x * (1.0 - 2.0 * gate))
    grad_m = exact(w_mix, w_out_t * silu1)
    bend = w_out_t * silu2
    coeffs = [exact(w_rad, grad_m)] + [exact(w_vec, 2.0 * v[c] * grad_m) for c in range(3)]

    low_lane = iota((1, 128), 1) < 64
    w_rad_hl = split2(w_rad)
    w_vec_hl = split2(w_vec)
    mix_hl = split2(w_mix)
    mix_t_hl = split2(w_mix_t)

    def dot_pre(a, b):
        b_high, b_low = split2(b)
        rows = a[0].shape[0]
        both = mm(jnp.concatenate(a, axis=0), b_high)
        return both[:rows] + (both[rows:] + mm(a[0], b_low))

    for kind in range(4):
        table = w_rad_t if kind == 0 else w_vec_t
        columns = [jnp.where(low_lane, table[:, 2 * m : 2 * m + 1], table[:, 2 * m + 1 : 2 * m + 2]) for m in range(4)]
        base = columns if kind == 0 else [2.0 * v[kind - 1] * column for column in columns]
        moved = jnp.concatenate(base, axis=1)
        bend4 = jnp.concatenate([bend] * 4, axis=1)
        shift = dot_pre(mix_hl, bend4 * dot_pre(mix_t_hl, moved))
        parts = [dot_pre(w_rad_hl, shift)]
        for c in range(3):
            term = jnp.concatenate([2.0 * v[c]] * 4, axis=1) * shift
            if kind == c + 1:
                term = term + jnp.concatenate([2.0 * grad_m * column for column in columns], axis=1)
            parts.append(dot_pre(w_vec_hl, term))
        block = jnp.concatenate(parts, axis=0)
        for m in range(4):
            piece = block[:, m * 128 : (m + 1) * 128]
            turned = pltpu.roll(piece, 64, 1)
            g_ref[kind * 8 + 2 * m] = jnp.where(low_lane, piece, turned)
            g_ref[kind * 8 + 2 * m + 1] = jnp.where(low_lane, turned, piece)

    def second_pass(hg, c):
        f, f1, f2 = fe_ref[hg, 0:8, :], fe_ref[hg, 8:16, :], fe_ref[hg, 24:32, :]
        h = [ms_ref[hg, b : b + 1, :] for b in range(3)]
        inv_r = ms_ref[hg, 3:4, :]
        r = 1.0 / inv_r

        def total(coeff, values):
            return jnp.sum(coeff * values, axis=0, keepdims=True)

        s2 = total(coeffs[0], f2)
        s1 = total(coeffs[0], f1)
        for b in range(3):
            psi, psi1, psi2 = (total(coeffs[b + 1], values) for values in (f, f1, f2))
            chi1 = (psi1 - psi * inv_r) * inv_r
            chi2 = (psi2 - 2.0 * chi1) * inv_r
            d_b = h[b] * r
            s2 = s2 + d_b * chi2
            s1 = s1 + d_b * chi1
            ms_ref[hg, 6 + b : 7 + b, :] = chi1
        s1 = s1 * inv_r
        ms_ref[hg, 4:5, :] = s2 - s1
        ms_ref[hg, 5:6, :] = s1
        return c

    lax.fori_loop(0, HALF_GROUPS, second_pass, 0, unroll=4)

    def wide(row):
        return jnp.broadcast_to(row, (8, 128))

    def change_of(ext):
        def gather(g, c):
            moved = mm(ext, d_ref[g])
            moved = moved[:96] + moved[96:]
            mv_ref[2 * g] = moved[:, :128].reshape(3, 4, 8, 128)
            mv_ref[2 * g + 1] = moved[:, 128:].reshape(3, 4, 8, 128)
            return c

        lax.fori_loop(0, GROUPS, gather, 0, unroll=True)

        def pair(p, c):
            for part in range(2):

                def edges(hg, acc):
                    h = [wide(ms_ref[hg, b : b + 1, :]) for b in range(3)]
                    inv_r = wide(ms_ref[hg, 3:4, :])
                    new = list(acc)
                    scaled, along, rho = [], [], []
                    for t in range(2):
                        u = [mv_ref[hg, b, 2 * p + t] for b in range(3)]
                        rho.append(h[0] * u[0] + h[1] * u[1] + h[2] * u[2])
                        scaled.append([u[b] * inv_r for b in range(3)])
                        along.append([h[b] * rho[t] for b in range(3)])
                    for k in range(4):
                        row = 4 * part + k
                        f = wide(fe_ref[hg, row : row + 1, :])
                        f1 = wide(fe_ref[hg, 8 + row : 9 + row, :])
                        e = wide(fe_ref[hg, 16 + row : 17 + row, :])
                        for t in range(2):
                            new[16 * t + k] = acc[16 * t + k] + f1 * rho[t]
                            for b in range(3):
                                at = 16 * t + 4 * (b + 1) + k
                                new[at] = acc[at] + (f * scaled[t][b] + e * along[t][b])
                    return tuple(new)

                acc = lax.fori_loop(
                    0, HALF_GROUPS, edges, tuple(jnp.zeros((8, 128), F32) for _ in range(32)), unroll=2
                )
                for at in range(16):
                    first, second = acc[at], acc[16 + at]
                    first = first + pltpu.roll(first, 64, 1)
                    second = second + pltpu.roll(second, 64, 1)
                    dd_ref[p, 8 * (at // 4) + 4 * part + at % 4] = jnp.where(low_lane, first, second)
            return c

        lax.fori_loop(0, 2, pair, 0)

    def response():
        def pair(p, c):
            def one(j, acc):
                delta = dd_ref[p, j]
                return tuple(acc[i] + wide(g_ref[j, i : i + 1, :]) * delta for i in range(32))

            acc = lax.fori_loop(0, 32, one, tuple(jnp.zeros((8, 128), F32) for _ in range(32)), unroll=2)
            for i in range(32):
                turned = pltpu.roll(acc[i], 64, 1)
                cf_ref[2 * p, i] = jnp.where(low_lane, acc[i], turned)
                cf_ref[2 * p + 1, i] = jnp.where(low_lane, turned, acc[i])
            return c

        lax.fori_loop(0, 2, pair, 0)

    def forces(slot):
        def tile(tt, c):
            a = [cf_ref[tt, i] for i in range(32)]

            def edges(hg, c2):
                u = [mv_ref[hg, b, tt] for b in range(3)]
                h = [wide(ms_ref[hg, b : b + 1, :]) for b in range(3)]
                inv_r = wide(ms_ref[hg, 3:4, :])
                alpha = wide(ms_ref[hg, 4:5, :])
                beta = wide(ms_ref[hg, 5:6, :])
                chi = [wide(ms_ref[hg, 6 + b : 7 + b, :]) for b in range(3)]
                rho = h[0] * u[0] + h[1] * u[1] + h[2] * u[2]
                level = alpha * rho + (chi[0] * u[0] + chi[1] * u[1] + chi[2] * u[2])
                across = [None] * 3
                along = [None] * 3
                for k in range(8):
                    f = wide(fe_ref[hg, k : k + 1, :])
                    f1 = wide(fe_ref[hg, 8 + k : 9 + k, :])
                    e = wide(fe_ref[hg, 16 + k : 17 + k, :])
                    level = level + f1 * a[k]
                    for b in range(3):
                        coeff = a[8 * (b + 1) + k]
                        across[b] = f * coeff if k == 0 else across[b] + f * coeff
                        along[b] = e * coeff if k == 0 else along[b] + e * coeff
                level = level + (h[0] * along[0] + h[1] * along[1] + h[2] * along[2])
                for b in range(3):
                    mv_ref[hg, b, tt] = inv_r * across[b] + beta * u[b] + h[b] * level + chi[b] * rho
                return c2

            lax.fori_loop(0, HALF_GROUPS, edges, 0, unroll=2)
            return c

        lax.fori_loop(0, 4, tile, 0)

        def scatter(g, acc):
            edge = jnp.concatenate([mv_ref[2 * g].reshape(96, 128), mv_ref[2 * g + 1].reshape(96, 128)], axis=1)
            high, low = split2(edge)
            return acc + mm_t(jnp.concatenate([high, low], axis=0), d_ref[g])

        both = lax.fori_loop(0, GROUPS, scatter, jnp.zeros((192, EXTENDED), F32), unroll=True)
        high, low = split2(both[:96] + both[96:])
        raw = mm_t(jnp.concatenate([high, low], axis=0), sel_ref[...])
        raw = raw[:96] + raw[96:]
        for i in range(9):
            part = raw[:, i * ATOMS : (i + 1) * ATOMS]
            for c in range(3):
                top, bottom = part[c * 32 : c * 32 + 16], part[c * 32 + 16 : c * 32 + 32]
                fold_send[slot, i, c * 16 : (c + 1) * 16, :] = jnp.concatenate([top, bottom], axis=1)

    def folded(slot):
        total = fold_send[slot, 4]
        for i in range(9):
            if i != 4:
                total = total + fold_recv[slot, i]
        return total

    def keep_rows(at, packed):
        for h in range(2):
            z_ref[at + h * 16 : at + h * 16 + 16, :] = jnp.concatenate(
                [packed[c * 16 : (c + 1) * 16, h * ATOMS : (h + 1) * ATOMS] for c in range(3)], axis=1
            )

    change_of(newer_ext)
    response()
    forces(0)
    start_all(fold_w)

    wait_all(older)
    change_of(extend(recv_p))
    keep_rows(96, recv_n[4, 0:48, :])
    keep_rows(128, recv_p[4])

    wait_all(fold_w)
    recv_w[4] = folded(0)
    start_all(work)

    response()
    forces(1)
    start_all(fold_q)
    keep_rows(32, recv_w[4])

    wait_all(work)
    change_of(extend(recv_w))
    response()
    forces(2)
    start_all(fold_y)

    wait_all(fold_q)
    keep_rows(64, folded(1))
    wait_all(fold_y)
    keep_rows(0, folded(2) * shrink)

    y_rows, w_rows, q_rows = z_ref[0:32, :], z_ref[32:64, :], z_ref[64:96, :]
    n_rows, p_rows = z_ref[96:128, :], z_ref[128:160, :]
    none = jnp.zeros((32, 192), F32)
    pay_ref[:, 0, :] = dot3_t(w_rows, jnp.concatenate([w_rows, n_rows, p_rows, q_rows], axis=0))
    pay_ref[:, 1, :] = dot3_t(y_rows, jnp.concatenate([y_rows, w_rows, q_rows, none], axis=0))
    pay_ref[:, 2, :] = dot3_t(p_rows, jnp.concatenate([p_rows, n_rows, q_rows, none], axis=0))
    pay_ref[:, 3, :] = dot3_t(n_rows, jnp.concatenate([n_rows, none, none, none], axis=0)) + dot3_t(
        q_rows, jnp.concatenate([none, q_rows, none, none], axis=0)
    )

    def slice_of(ref, r):
        return ref.at[pl.ds(r * rpd, rpd)]

    def stage0(dy, flip):
        peer, device = plane_peer(dy, flip)
        slot = 2 * dy + int(flip)
        return pltpu.make_async_remote_copy(
            src_ref=slice_of(pay_ref, peer),
            dst_ref=rs_ref.at[me],
            send_sem=ar_send.at[0, slot],
            recv_sem=ar_recv.at[0, slot],
            device_id=device,
            device_id_type=MESH,
        )

    def stage1(dz):
        return pltpu.make_async_remote_copy(
            src_ref=zs_ref.at[z_pos],
            dst_ref=zs_ref.at[z_pos],
            send_sem=ar_send.at[1, dz],
            recv_sem=ar_recv.at[1, dz],
            device_id=line_peer(dz),
            device_id_type=MESH,
        )

    def stage2(dy, flip):
        slot = 2 * dy + int(flip)
        return pltpu.make_async_remote_copy(
            src_ref=slice_of(tot_ref, me),
            dst_ref=slice_of(tot_ref, me),
            send_sem=ar_send.at[2, slot],
            recv_sem=ar_recv.at[2, slot],
            device_id=plane_peer(dy, flip)[1],
            device_id_type=MESH,
        )

    def run(make, each):
        each(lambda *peer: make(*peer).start())
        each(lambda *peer: make(*peer).wait())

    rs_ref[me] = pay_ref[pl.ds(me * rpd, rpd)]
    run(stage0, each_plane)
    zs_ref[z_pos] = jnp.sum(rs_ref[...], axis=0)
    run(stage1, each_line)
    tot_ref[pl.ds(me * rpd, rpd)] = jnp.sum(zs_ref[...], axis=0) * (1.0 / total_rows)
    run(stage2, each_plane)

    g1, g2, g3, g4 = (tot_ref[:, j, :] for j in range(4))
    t1, t2, t3 = (jnp.transpose(g) for g in (g1, g2, g3))

    def block(source, i):
        return source[:, i * 32 : (i + 1) * 32]

    def tblock(source, i):
        return source[i * 32 : (i + 1) * 32]

    ww, wn, wp, wq = (block(g1, i) for i in range(4))
    wq_s, ww_s, qw = wq * shrink, ww * shrink, tblock(t1, 3)
    column_y = jnp.concatenate([block(g2, 0), tblock(t2, 1), tblock(t2, 2), ww_s, qw * shrink], axis=0)
    column_w = jnp.concatenate([block(g2, 1), ww, qw, tblock(t1, 1), tblock(t1, 2)], axis=0)
    column_q = jnp.concatenate([block(g2, 2), wq, block(g4, 1), wp, block(g3, 2)], axis=0)
    column_n = jnp.concatenate([ww_s, wn, tblock(t1, 2), block(g4, 0), block(g3, 1)], axis=0)
    column_p = jnp.concatenate([wq_s, wp, tblock(t3, 2), tblock(t3, 1), block(g3, 0)], axis=0)
    gram = jnp.concatenate([column_y, column_w, column_q, column_n, column_p], axis=1)

    eye = (iota((32, 32), 0) == iota((32, 32), 1)).astype(F32)
    zero = jnp.zeros((32, 32), F32)
    resid1 = jnp.concatenate([zero, eye, zero, -wn, -wp], axis=1)
    image1 = jnp.concatenate([eye * grow, -wn, -wp, zero, zero], axis=1)
    lower1, inverse1 = factor_and_inverse(exact_t(exact(resid1, gram), resid1))
    fresh1 = exact(inverse1, resid1)
    work2 = exact(inverse1, image1)
    product = exact(work2, gram)
    on_newer = iota((32, 160), 1) // 32 == 3
    resid2 = work2 - exact(exact_t(product, fresh1), fresh1) - jnp.where(on_newer, product, 0.0)
    lower2, inverse2 = factor_and_inverse(exact_t(exact(resid2, gram), resid2))
    fresh2 = exact(inverse2, resid2)
    fac_ref[0] = lower1
    fac_ref[1] = lower2
    fresh = dot3(jnp.concatenate([fresh1, fresh2], axis=0), z_ref[...])
    for s in range(2):
        for c in range(3):
            out_ref[s, c] = fresh[s * 32 : (s + 1) * 32, c * ATOMS : (c + 1) * ATOMS]


def shards(n_gx, n_gy, positions, block_prev, block_cur, neighbours, counts, x_lists, y_lists, w_radial, w_vector, w_mix, w_out):
    n_z, plane = n_gx // 2, 2 * n_gy
    rpd = 32 // plane
    total_rows = 3.0 * ATOMS * n_gx * n_gy
    vmem = pl.BlockSpec(memory_space=pltpu.VMEM)
    blocks, factors = pl.pallas_call(
        functools.partial(kernel, n_gx, n_gy, total_rows),
        out_shape=(
            jax.ShapeDtypeStruct((2, 3, VECTORS, ATOMS), F32),
            jax.ShapeDtypeStruct((2, VECTORS, VECTORS), F32),
        ),
        in_specs=[vmem] * 11,
        out_specs=(vmem, vmem),
        scratch_shapes=[
            pltpu.VMEM((9, META + 8, 128), F32),
            pltpu.VMEM((9, 48, 128), F32),
            pltpu.VMEM((9, 48, 128), F32),
            pltpu.VMEM((3, 9, 48, 128), F32),
            pltpu.VMEM((3, 9, 48, 128), F32),
            pltpu.VMEM((GROUPS, EXTENDED, 256), BF16),
            pltpu.VMEM((RAW, EXTENDED), BF16),
            pltpu.VMEM((HALF_GROUPS, 32, 128), F32),
            pltpu.VMEM((HALF_GROUPS, 16, 128), F32),
            pltpu.VMEM((HALF_GROUPS, 3, 4, 8, 128), F32),
            pltpu.VMEM((2, 32, 8, 128), F32),
            pltpu.VMEM((4, 32, 8, 128), F32),
            pltpu.VMEM((32, 32, 128), F32),
            pltpu.VMEM((160, 192), F32),
            pltpu.VMEM((32, 4, 128), F32),
            pltpu.VMEM((plane, rpd, 4, 128), F32),
            pltpu.VMEM((n_z, rpd, 4, 128), F32),
            pltpu.VMEM((32, 4, 128), F32),
            pltpu.SemaphoreType.DMA((6, 9)),
            pltpu.SemaphoreType.DMA((6, 9)),
            pltpu.SemaphoreType.DMA((3, 32)),
            pltpu.SemaphoreType.DMA((3, 32)),
        ],
        compiler_params=pltpu.CompilerParams(collective_id=0, has_side_effects=True),
    )(
        positions,
        jnp.transpose(block_prev, (1, 0, 2)),
        jnp.transpose(block_cur, (1, 0, 2)),
        neighbours,
        counts.reshape(1, ATOMS),
        x_lists,
        y_lists,
        w_radial,
        w_vector,
        w_mix,
        w_out.reshape(1, 128),
    )
    return jnp.transpose(blocks, (0, 2, 1, 3)), factors


def solution(mesh):
    placed = (
        P(None, ("gx", "gy")),
        P(None, None, ("gx", "gy")),
        P(None, None, ("gx", "gy")),
        P(None, ("gx", "gy")),
        P(("gx", "gy")),
        P(("gx", "gy"), None, None),
        P(("gx", "gy"), None, None),
        P(),
        P(),
        P(),
        P(),
    )
    return jax.shard_map(
        functools.partial(shards, mesh.shape["gx"], mesh.shape["gy"]),
        mesh=mesh,
        in_specs=placed,
        out_specs=(P(None, None, None, ("gx", "gy")), P()),
        check_vma=False,
    )
```

```python
import functools

import jax
import jax.numpy as jnp
from jax import lax
from jax.experimental import pallas as pl
from jax.experimental.pallas import tpu as pltpu
from jax.sharding import PartitionSpec as P

MESH = pl.DeviceIdType.MESH
F32 = jnp.float32
BF16 = jnp.bfloat16
HIGHEST = lax.Precision.HIGHEST

VECTORS = 32
SLOTS = 32
ATOMS = 64
EXTENDED = 320
RAW = 576
SOFTEN = 0.25
CUTOFF = 5.0
BASIS_SIZE = 8
GROUPS = SLOTS // 4
HALF_GROUPS = 2 * GROUPS
PIVOTS = 4

EX_NEWER, EX_OLDER, EX_FOLD_W, EX_WORK, EX_FOLD_Q, EX_FOLD_Y, EX_META = range(7)


def split2(x):
    high = x.astype(BF16)
    low = (x - high.astype(F32)).astype(BF16)
    return high, low


def mm(a, b):
    return jnp.dot(a, b, preferred_element_type=F32)


def mm_t(a, b):
    return lax.dot_general(a, b, (((1,), (1,)), ((), ())), preferred_element_type=F32)


def dot3(a, b):
    a_high, a_low = split2(a)
    b_high, b_low = split2(b)
    return mm(a_high, b_high) + (mm(a_high, b_low) + mm(a_low, b_high))


def dot3_t(a, b):
    a_high, a_low = split2(a)
    b_high, b_low = split2(b)
    return mm_t(a_high, b_high) + (mm_t(a_high, b_low) + mm_t(a_low, b_high))


def exact(a, b):
    return jnp.dot(a, b, precision=HIGHEST, preferred_element_type=F32)


def iota(shape, axis):
    return lax.broadcasted_iota(jnp.int32, shape, axis)


def factor_and_inverse(gram):
    n = gram.shape[0]
    row, column = iota((n, n), 0), iota((n, n), 1)
    wide_row = iota((n, 2 * n), 0)
    state = jnp.concatenate([gram, (row == column).astype(F32)], axis=1)
    lower = jnp.zeros((n, n), F32)
    for j in range(0, n, PIVOTS):
        at = [slice(j + p, j + p + 1) for p in range(PIVOTS)]
        small, scale, rows, columns = [], [], [], []
        for p in range(PIVOTS):
            entries = []
            for q in range(p):
                entry = state[at[p], at[q]]
                for m in range(q):
                    entry = entry - entries[m] * small[q][m]
                entries.append(entry * scale[q])
            pivot = state[at[p], at[p]]
            for m in range(p):
                pivot = pivot - entries[m] * entries[m]
            small.append(entries)
            scale.append(lax.rsqrt(pivot))
        for p in range(PIVOTS):
            pivot_row, pivot_column = state[at[p], :], state[:, at[p]]
            for m in range(p):
                pivot_row = pivot_row - small[p][m] * rows[m]
                pivot_column = pivot_column - small[p][m] * columns[m]
            rows.append(pivot_row * scale[p])
            columns.append(pivot_column * scale[p])
        below = state
        for p in range(PIVOTS):
            below = below - columns[p] * rows[p]
            lower = jnp.where((column == j + p) & (row >= j + p), columns[p], lower)
        state = jnp.where(wide_row >= j + PIVOTS, below, state)
        for p in range(PIVOTS):
            state = jnp.where(wide_row == j + p, rows[p], state)
    return lower, state[:, n:]


def kernel(
    n_gx,
    n_gy,
    total_rows,
    pos_ref,
    prev_ref,
    cur_ref,
    nb_ref,
    cnt_ref,
    xl_ref,
    yl_ref,
    wr_ref,
    wv_ref,
    wmix_ref,
    wout_ref,
    out_ref,
    fac_ref,
    recv_m,
    recv_n,
    recv_p,
    recv_w,
    fold_send,
    fold_recv,
    d_ref,
    sel_ref,
    fe_ref,
    ms_ref,
    mv_ref,
    dd_ref,
    cf_ref,
    g_ref,
    z_ref,
    pay_ref,
    rs_ref,
    zs_ref,
    tot_ref,
    ex_send,
    ex_recv,
    ar_send,
    ar_recv,
):
    n_z = n_gx // 2
    plane = 2 * n_gy
    rpd = 32 // plane
    gx = lax.axis_index("gx")
    gy = lax.axis_index("gy")
    z_pos, core = gx // 2, gx % 2
    me = gy * 2 + core

    def wrapped(value, size):
        return jnp.where(value >= size, value - size, value)

    gx_near = (wrapped(gx + (n_gx - 1), n_gx), gx, wrapped(gx + 1, n_gx))
    gy_near = (wrapped(gy + (n_gy - 1), n_gy), gy, wrapped(gy + 1, n_gy))
    others = [i for i in range(9) if i != 4]

    def near(i):
        return gx_near[i // 3], gy_near[i % 3]

    def plane_peer(dy, flip):
        to_y = wrapped(gy + dy, n_gy)
        to_core = 1 - core if flip else core
        return to_y * 2 + to_core, (z_pos * 2 + to_core, to_y)

    def line_peer(dz):
        return wrapped(z_pos + dz, n_z) * 2 + core, gy

    def each_plane(act):
        act(0, True)

        def body(d, c):
            dy = d + n_gy // 2
            dy = jnp.where(dy >= n_gy, dy - (n_gy - 1), dy)
            act(dy, False)
            act(dy, True)
            return c

        lax.fori_loop(1, n_gy, body, 0)

    def each_line(act):
        def body(d, c):
            dz = d + n_z // 2 - 1
            dz = jnp.where(dz >= n_z, dz - (n_z - 1), dz)
            act(dz)
            return c

        lax.fori_loop(1, n_z, body, 0)

    barrier = pltpu.get_barrier_semaphore()

    def greet(device):
        pl.semaphore_signal(barrier, inc=1, device_id=device, device_id_type=MESH)

    for i in others:
        greet(near(i))
    each_line(lambda dz: greet(line_peer(dz)))
    each_plane(lambda dy, flip: greet(plane_peer(dy, flip)[1]))

    def pack_own(source, target):
        for c in range(3):
            block = source[c]
            target[4, c * 16 : (c + 1) * 16, :] = jnp.concatenate([block[:16], block[16:]], axis=1)

    pack_own(cur_ref, recv_n)
    pack_own(prev_ref, recv_p)
    left = jnp.concatenate([pos_ref[...], jnp.zeros((5, ATOMS), F32)], axis=0)
    right = jnp.concatenate(
        [xl_ref[0].astype(F32), yl_ref[0].astype(F32), jnp.zeros((4, ATOMS), F32)], axis=0
    )
    recv_m[4] = jnp.concatenate([left, right], axis=1)

    pl.semaphore_wait(barrier, 8 + (n_z - 1) + (plane - 1))

    def spread_copy(number, ref, i):
        return pltpu.make_async_remote_copy(
            src_ref=ref.at[4],
            dst_ref=ref.at[8 - i],
            send_sem=ex_send.at[number, i],
            recv_sem=ex_recv.at[number, 8 - i],
            device_id=near(i),
            device_id_type=MESH,
        )

    def fold_copy(number, slot, i):
        return pltpu.make_async_remote_copy(
            src_ref=fold_send.at[slot, i],
            dst_ref=fold_recv.at[slot, 8 - i],
            send_sem=ex_send.at[number, i],
            recv_sem=ex_recv.at[number, 8 - i],
            device_id=near(i),
            device_id_type=MESH,
        )

    def start_all(make):
        for i in others:
            make(i).start()

    def wait_all(make):
        for i in others:
            make(i).wait()

    meta = functools.partial(spread_copy, EX_META, recv_m)
    newer = functools.partial(spread_copy, EX_NEWER, recv_n)
    older = functools.partial(spread_copy, EX_OLDER, recv_p)
    work = functools.partial(spread_copy, EX_WORK, recv_w)
    fold_w = functools.partial(fold_copy, EX_FOLD_W, 0)
    fold_q = functools.partial(fold_copy, EX_FOLD_Q, 1)
    fold_y = functools.partial(fold_copy, EX_FOLD_Y, 2)
    start_all(meta)
    start_all(newer)
    start_all(older)

    count_row = cnt_ref[...]
    count_row = jnp.concatenate([count_row] * 4, axis=1)
    lane = iota((1, 256), 1)

    def build_incidence(g, c):
        rows = [nb_ref[pl.ds(4 * g + s, 1), :] for s in range(4)]
        index = jnp.concatenate(rows, axis=1)
        valid = (4 * g + lane // ATOMS) < count_row
        index = jnp.where(valid, index, -1)
        own = jnp.where(valid, lane % ATOMS, -1)
        picked = (iota((EXTENDED, 256), 0) == index).astype(F32)
        minus = (iota((ATOMS, 256), 0) == own).astype(F32)
        d_ref[g] = jnp.concatenate([picked[:ATOMS] - minus, picked[ATOMS:]], axis=0).astype(BF16)
        return c

    lax.fori_loop(0, GROUPS, build_incidence, 0)

    w_vec = wv_ref[...]
    w_rad = wr_ref[...]
    w_mix = wmix_ref[...]
    w_mix_t = jnp.transpose(w_mix)
    pad = jnp.zeros((112, 128), F32)
    w_both_t = jnp.transpose(jnp.concatenate([w_rad, w_vec, pad], axis=0))
    w_rad_t = w_both_t[:, :8]
    w_vec_t = w_both_t[:, 8:16]
    w_out_t = jnp.transpose(jnp.broadcast_to(wout_ref[...], (128, 128)))
    level = jnp.sqrt(jnp.sum(wout_ref[...] * wout_ref[...])) * jnp.sqrt(jnp.sum(w_mix * w_mix)) * jnp.sum(w_vec * w_vec)
    shrink = 1.0 / jnp.clip(level, 1e-8, 1e8)
    grow = jnp.clip(level, 1e-8, 1e8)

    def raw_rows(ref):
        pieces = []
        for c in range(3):
            for h in range(2):
                pieces.append(
                    jnp.concatenate(
                        [ref[i, c * 16 : (c + 1) * 16, h * ATOMS : (h + 1) * ATOMS] for i in range(9)], axis=1
                    )
                )
        return jnp.concatenate(pieces, axis=0)

    def extend(ref):
        high, low = split2(raw_rows(ref))
        return mm(jnp.concatenate([high, low], axis=0), sel_ref[...]).astype(BF16)

    wait_all(meta)

    def listed(slot, row):
        return recv_m[slot, row : row + 1, ATOMS:]

    own_row = iota((1, ATOMS), 1).astype(F32)

    def widened(own_slot, left_slot, right_slot):
        return jnp.concatenate(
            [own_row + own_slot * 64.0, listed(left_slot, 0) + left_slot * 64.0, listed(right_slot, 1) + right_slot * 64.0],
            axis=1,
        )

    def looked_up(table, picks):
        hot = (iota((3 * ATOMS, ATOMS), 0).astype(F32) == picks).astype(F32)
        return exact(jnp.broadcast_to(table, (8, 3 * ATOMS)), hot)[0:1]

    before = looked_up(widened(3, 0, 6), listed(3, 2))
    after = looked_up(widened(5, 2, 8), listed(5, 3))
    to_raw = jnp.concatenate([widened(4, 1, 7), before, after], axis=1)
    to_raw = (to_raw + 0.5).astype(jnp.int32)
    sel_ref[...] = (iota((RAW, EXTENDED), 0) == to_raw).astype(F32).astype(BF16)

    raw_pos = jnp.concatenate([recv_m[i, :, :ATOMS] for i in range(9)], axis=1)
    p_high = raw_pos.astype(BF16)
    rest = raw_pos - p_high.astype(F32)
    p_mid = rest.astype(BF16)
    p_low = (rest - p_mid.astype(F32)).astype(BF16)
    zero8 = jnp.zeros((8, RAW), BF16)
    pos_ext = mm(jnp.concatenate([p_high, p_mid, p_low, zero8], axis=0), sel_ref[...]).astype(BF16)

    center = CUTOFF * (iota((BASIS_SIZE, 1), 0).astype(F32) + 0.5) / BASIS_SIZE
    descriptor = [jnp.zeros((BASIS_SIZE, 256), F32) for _ in range(4)]

    def edge_rows(g):
        parts = mm(pos_ext, d_ref[g])
        d = parts[0:8] + (parts[8:16] + parts[16:24])
        d = d[0:3]
        squared = jnp.sum(d * d, axis=0, keepdims=True) + SOFTEN
        inv_r = lax.rsqrt(squared)
        r = squared * inv_r
        h = d * inv_r
        q = jnp.maximum(1.0 - squared * (1.0 / (CUTOFF * CUTOFF)), 0.0)
        env = q * q * q
        env1 = (-6.0 / 25.0) * r * q * q
        env2 = (-6.0 / 25.0) * q * q + (24.0 / 625.0) * squared * q
        offset = r - center
        bell = jnp.exp(-2.0 * offset * offset)
        f = bell * env
        f1 = bell * (env1 - 4.0 * offset * env)
        f2 = bell * (env2 - 8.0 * offset * env1 + (16.0 * offset * offset - 4.0) * env)
        return d, h, inv_r, f, f1, f2

    def first_pass(g, descriptor):
        d, h, inv_r, f, f1, f2 = edge_rows(g)
        valid = ((4 * g + lane // ATOMS) < count_row).astype(F32)
        e = f1 - f * inv_r
        for half in range(2):
            cut = slice(half * 128, (half + 1) * 128)
            fe_ref[2 * g + half, 0:8, :] = f[:, cut]
            fe_ref[2 * g + half, 8:16, :] = f1[:, cut]
            fe_ref[2 * g + half, 16:24, :] = e[:, cut]
            ms_ref[2 * g + half, 0:3, :] = h[:, cut]
            ms_ref[2 * g + half, 3:4, :] = inv_r[:, cut]
            fe_ref[2 * g + half, 24:32, :] = f2[:, cut]
        masked = f * valid
        return (
            descriptor[0] + masked,
            descriptor[1] + masked * h[0:1],
            descriptor[2] + masked * h[1:2],
            descriptor[3] + masked * h[2:3],
        )

    descriptor = lax.fori_loop(0, GROUPS, first_pass, tuple(descriptor), unroll=True)

    def fold_lanes(x):
        x = x[:, :128] + x[:, 128:]
        return x + pltpu.roll(x, 64, 1)

    descriptor = [fold_lanes(x) for x in descriptor]

    v = [dot3(w_vec_t, descriptor[c + 1]) for c in range(3)]
    mixed_in = dot3(w_rad_t, descriptor[0]) + (v[0] * v[0] + v[1] * v[1] + v[2] * v[2])
    x = dot3(w_mix_t, mixed_in)
    gate = jax.nn.sigmoid(x)
    slope = gate * (1.0 - gate)
    silu1 = gate + x * slope
    silu2 = slope * (2.0 + x * (1.0 - 2.0 * gate))
    grad_m = dot3(w_mix, w_out_t * silu1)
    bend = w_out_t * silu2
    coeffs = [dot3(w_rad, grad_m)] + [dot3(w_vec, 2.0 * v[c] * grad_m) for c in range(3)]

    low_lane = iota((1, 128), 1) < 64
    w_rad_hl = split2(w_rad)
    w_vec_hl = split2(w_vec)
    mix_hl = split2(w_mix)
    mix_t_hl = split2(w_mix_t)

    def dot_pre(a, b):
        b_high, b_low = split2(b)
        rows = a[0].shape[0]
        both = mm(jnp.concatenate(a, axis=0), b_high)
        return both[:rows] + (both[rows:] + mm(a[0], b_low))

    for kind in range(4):
        table = w_rad_t if kind == 0 else w_vec_t
        columns = [jnp.where(low_lane, table[:, 2 * m : 2 * m + 1], table[:, 2 * m + 1 : 2 * m + 2]) for m in range(4)]
        base = columns if kind == 0 else [2.0 * v[kind - 1] * column for column in columns]
        moved = jnp.concatenate(base, axis=1)
        bend4 = jnp.concatenate([bend] * 4, axis=1)
        shift = dot_pre(mix_hl, bend4 * dot_pre(mix_t_hl, moved))
        parts = [dot_pre(w_rad_hl, shift)]
        for c in range(3):
            term = jnp.concatenate([2.0 * v[c]] * 4, axis=1) * shift
            if kind == c + 1:
                term = term + jnp.concatenate([2.0 * grad_m * column for column in columns], axis=1)
            parts.append(dot_pre(w_vec_hl, term))
        block = jnp.concatenate(parts, axis=0)
        for m in range(4):
            piece = block[:, m * 128 : (m + 1) * 128]
            turned = pltpu.roll(piece, 64, 1)
            g_ref[kind * 8 + 2 * m] = jnp.where(low_lane, piece, turned)
            g_ref[kind * 8 + 2 * m + 1] = jnp.where(low_lane, turned, piece)

    def second_pass(hg, c):
        f, f1, f2 = fe_ref[hg, 0:8, :], fe_ref[hg, 8:16, :], fe_ref[hg, 24:32, :]
        h = [ms_ref[hg, b : b + 1, :] for b in range(3)]
        inv_r = ms_ref[hg, 3:4, :]
        r = 1.0 / inv_r

        def total(coeff, values):
            return jnp.sum(coeff * values, axis=0, keepdims=True)

        s2 = total(coeffs[0], f2)
        s1 = total(coeffs[0], f1)
        for b in range(3):
            psi, psi1, psi2 = (total(coeffs[b + 1], values) for values in (f, f1, f2))
            chi1 = (psi1 - psi * inv_r) * inv_r
            chi2 = (psi2 - 2.0 * chi1) * inv_r
            d_b = h[b] * r
            s2 = s2 + d_b * chi2
            s1 = s1 + d_b * chi1
            ms_ref[hg, 6 + b : 7 + b, :] = chi1
        s1 = s1 * inv_r
        ms_ref[hg, 4:5, :] = s2 - s1
        ms_ref[hg, 5:6, :] = s1
        return c

    lax.fori_loop(0, HALF_GROUPS, second_pass, 0, unroll=4)

    def wide(row):
        return jnp.broadcast_to(row, (8, 128))

    def change_of(ext):
        def gather(g, c):
            moved = mm(ext, d_ref[g])
            moved = moved[:96] + moved[96:]
            mv_ref[2 * g] = moved[:, :128].reshape(3, 4, 8, 128)
            mv_ref[2 * g + 1] = moved[:, 128:].reshape(3, 4, 8, 128)
            return c

        lax.fori_loop(0, GROUPS, gather, 0, unroll=True)

        def pair(p, c):
            for part in range(2):

                def edges(hg, acc):
                    h = [wide(ms_ref[hg, b : b + 1, :]) for b in range(3)]
                    inv_r = wide(ms_ref[hg, 3:4, :])
                    new = list(acc)
                    scaled, along, rho = [], [], []
                    for t in range(2):
                        u = [mv_ref[hg, b, 2 * p + t] for b in range(3)]
                        rho.append(h[0] * u[0] + h[1] * u[1] + h[2] * u[2])
                        scaled.append([u[b] * inv_r for b in range(3)])
                        along.append([h[b] * rho[t] for b in range(3)])
                    for k in range(4):
                        row = 4 * part + k
                        f = wide(fe_ref[hg, row : row + 1, :])
                        f1 = wide(fe_ref[hg, 8 + row : 9 + row, :])
                        e = wide(fe_ref[hg, 16 + row : 17 + row, :])
                        for t in range(2):
                            new[16 * t + k] = acc[16 * t + k] + f1 * rho[t]
                            for b in range(3):
                                at = 16 * t + 4 * (b + 1) + k
                                new[at] = acc[at] + (f * scaled[t][b] + e * along[t][b])
                    return tuple(new)

                acc = lax.fori_loop(
                    0, HALF_GROUPS, edges, tuple(jnp.zeros((8, 128), F32) for _ in range(32)), unroll=2
                )
                for at in range(16):
                    first, second = acc[at], acc[16 + at]
                    first = first + pltpu.roll(first, 64, 1)
                    second = second + pltpu.roll(second, 64, 1)
                    dd_ref[p, 8 * (at // 4) + 4 * part + at % 4] = jnp.where(low_lane, first, second)
            return c

        lax.fori_loop(0, 2, pair, 0)

    def response():
        def pair(p, c):
            def one(j, acc):
                delta = dd_ref[p, j]
                return tuple(acc[i] + wide(g_ref[j, i : i + 1, :]) * delta for i in range(32))

            acc = lax.fori_loop(0, 32, one, tuple(jnp.zeros((8, 128), F32) for _ in range(32)), unroll=2)
            for i in range(32):
                turned = pltpu.roll(acc[i], 64, 1)
                cf_ref[2 * p, i] = jnp.where(low_lane, acc[i], turned)
                cf_ref[2 * p + 1, i] = jnp.where(low_lane, turned, acc[i])
            return c

        lax.fori_loop(0, 2, pair, 0)

    def forces(slot):
        def tile(tt, c):
            a = [cf_ref[tt, i] for i in range(32)]

            def edges(hg, c2):
                u = [mv_ref[hg, b, tt] for b in range(3)]
                h = [wide(ms_ref[hg, b : b + 1, :]) for b in range(3)]
                inv_r = wide(ms_ref[hg, 3:4, :])
                alpha = wide(ms_ref[hg, 4:5, :])
                beta = wide(ms_ref[hg, 5:6, :])
                chi = [wide(ms_ref[hg, 6 + b : 7 + b, :]) for b in range(3)]
                rho = h[0] * u[0] + h[1] * u[1] + h[2] * u[2]
                level = alpha * rho + (chi[0] * u[0] + chi[1] * u[1] + chi[2] * u[2])
                across = [None] * 3
                along = [None] * 3
                for k in range(8):
                    f = wide(fe_ref[hg, k : k + 1, :])
                    f1 = wide(fe_ref[hg, 8 + k : 9 + k, :])
                    e = wide(fe_ref[hg, 16 + k : 17 + k, :])
                    level = level + f1 * a[k]
                    for b in range(3):
                        coeff = a[8 * (b + 1) + k]
                        across[b] = f * coeff if k == 0 else across[b] + f * coeff
                        along[b] = e * coeff if k == 0 else along[b] + e * coeff
                level = level + (h[0] * along[0] + h[1] * along[1] + h[2] * along[2])
                for b in range(3):
                    mv_ref[hg, b, tt] = inv_r * across[b] + beta * u[b] + h[b] * level + chi[b] * rho
                return c2

            lax.fori_loop(0, HALF_GROUPS, edges, 0, unroll=2)
            return c

        lax.fori_loop(0, 4, tile, 0)

        def scatter(g, acc):
            edge = jnp.concatenate([mv_ref[2 * g].reshape(96, 128), mv_ref[2 * g + 1].reshape(96, 128)], axis=1)
            high, low = split2(edge)
            return acc + mm_t(jnp.concatenate([high, low], axis=0), d_ref[g])

        both = lax.fori_loop(0, GROUPS, scatter, jnp.zeros((192, EXTENDED), F32), unroll=True)
        high, low = split2(both[:96] + both[96:])
        raw = mm_t(jnp.concatenate([high, low], axis=0), sel_ref[...])
        raw = raw[:96] + raw[96:]
        for i in range(9):
            part = raw[:, i * ATOMS : (i + 1) * ATOMS]
            for c in range(3):
                top, bottom = part[c * 32 : c * 32 + 16], part[c * 32 + 16 : c * 32 + 32]
                fold_send[slot, i, c * 16 : (c + 1) * 16, :] = jnp.concatenate([top, bottom], axis=1)

    def folded(slot):
        total = fold_send[slot, 4]
        for i in range(9):
            if i != 4:
                total = total + fold_recv[slot, i]
        return total

    def keep_rows(at, packed):
        for h in range(2):
            z_ref[at + h * 16 : at + h * 16 + 16, :] = jnp.concatenate(
                [packed[c * 16 : (c + 1) * 16, h * ATOMS : (h + 1) * ATOMS] for c in range(3)], axis=1
            )

    def reduce_steps(n):
        def slice_of(ref, r):
            return ref.at[n, pl.ds(r * rpd, rpd)]

        def stage0(dy, flip):
            peer, device = plane_peer(dy, flip)
            slot = 2 * dy + int(flip)
            return pltpu.make_async_remote_copy(
                src_ref=slice_of(pay_ref, peer),
                dst_ref=rs_ref.at[n, me],
                send_sem=ar_send.at[3 * n, slot],
                recv_sem=ar_recv.at[3 * n, slot],
                device_id=device,
                device_id_type=MESH,
            )

        def stage1(dz):
            return pltpu.make_async_remote_copy(
                src_ref=zs_ref.at[n, z_pos],
                dst_ref=zs_ref.at[n, z_pos],
                send_sem=ar_send.at[3 * n + 1, dz],
                recv_sem=ar_recv.at[3 * n + 1, dz],
                device_id=line_peer(dz),
                device_id_type=MESH,
            )

        def stage2(dy, flip):
            slot = 2 * dy + int(flip)
            return pltpu.make_async_remote_copy(
                src_ref=slice_of(tot_ref, me),
                dst_ref=slice_of(tot_ref, me),
                send_sem=ar_send.at[3 * n + 2, slot],
                recv_sem=ar_recv.at[3 * n + 2, slot],
                device_id=plane_peer(dy, flip)[1],
                device_id_type=MESH,
            )

        def begin(make, each):
            each(lambda *peer: make(*peer).start())

        def end(make, each):
            each(lambda *peer: make(*peer).wait())

        def first():
            begin(stage0, each_plane)
            rs_ref[n, me] = pay_ref[n, pl.ds(me * rpd, rpd)]

        def second():
            end(stage0, each_plane)
            zs_ref[n, z_pos] = jnp.sum(rs_ref[n], axis=0)
            begin(stage1, each_line)

        def third():
            end(stage1, each_line)
            tot_ref[n, pl.ds(me * rpd, rpd)] = jnp.sum(zs_ref[n], axis=0) * (1.0 / total_rows)
            begin(stage2, each_plane)

        def last():
            end(stage2, each_plane)
            return tot_ref[n, :, 0, :], tot_ref[n, :, 1, :]

        return first, second, third, last

    def rows_of(at):
        return z_ref[at : at + 32, :]

    none = jnp.zeros((32, 192), F32)
    low1, low2, low3, low4 = reduce_steps(0)
    top1, top2, top3, top4 = reduce_steps(1)

    wait_all(newer)
    change_of(extend(recv_n))
    response()
    forces(0)
    start_all(fold_w)

    wait_all(older)
    change_of(extend(recv_p))
    response()
    keep_rows(96, recv_n[4])
    keep_rows(128, recv_p[4])
    n_rows, p_rows = rows_of(96), rows_of(128)
    pay_ref[0, :, 1, :] = dot3_t(n_rows, jnp.concatenate([n_rows, p_rows, none, none], axis=0)) + dot3_t(
        p_rows, jnp.concatenate([none, none, p_rows, none], axis=0)
    )

    wait_all(fold_w)
    recv_w[4] = folded(0)
    start_all(work)

    keep_rows(32, recv_w[4])
    w_rows = rows_of(32)
    pay_ref[0, :, 0, :] = dot3_t(w_rows, jnp.concatenate([w_rows, rows_of(96), rows_of(128), none], axis=0))
    low1()
    forces(1)
    start_all(fold_q)
    low2()

    wait_all(work)
    change_of(extend(recv_w))
    response()
    forces(2)
    start_all(fold_y)
    low3()

    wait_all(fold_q)
    keep_rows(64, folded(1))
    q_rows = rows_of(64)
    pay_ref[1, :, 1, :] = dot3_t(q_rows, jnp.concatenate([rows_of(32), rows_of(128), q_rows, none], axis=0))
    wait_all(fold_y)
    keep_rows(0, folded(2) * shrink)
    y_rows = rows_of(0)
    pay_ref[1, :, 0, :] = dot3_t(y_rows, jnp.concatenate([y_rows, rows_of(32), rows_of(64), none], axis=0))
    top1()

    def block(source, i):
        return source[:, i * 32 : (i + 1) * 32]

    def tblock(source, i):
        return source[i * 32 : (i + 1) * 32]

    g1, g2 = low4()
    t1, t2 = jnp.transpose(g1), jnp.transpose(g2)
    eye = (iota((32, 32), 0) == iota((32, 32), 1)).astype(F32)
    zero = jnp.zeros((32, 32), F32)
    ww, wn, wp = (block(g1, i) for i in range(3))
    nw, pw, pn = tblock(t1, 1), tblock(t1, 2), tblock(t2, 1)
    nn, np_, pp = (block(g2, i) for i in range(3))
    small = jnp.concatenate(
        [
            jnp.concatenate([ww, nw, pw], axis=0),
            jnp.concatenate([wn, nn, pn], axis=0),
            jnp.concatenate([wp, np_, pp], axis=0),
        ],
        axis=1,
    )
    resid1 = jnp.concatenate([eye, -wn, -wp], axis=1)
    lower1, inverse1 = factor_and_inverse(dot3_t(dot3(resid1, small), resid1))
    fac_ref[0] = lower1
    fresh1 = dot3(inverse1, resid1)
    f_w, f_n, f_p = (block(fresh1, i) for i in range(3))
    fresh1 = jnp.concatenate([zero, f_w, zero, f_n, f_p], axis=1)
    work2 = jnp.concatenate([inverse1 * grow, f_n, f_p, zero, zero], axis=1)
    top2()

    def write(s, coefficients):
        fresh = dot3(coefficients, z_ref[...])
        for c in range(3):
            out_ref[s, c] = fresh[:, c * ATOMS : (c + 1) * ATOMS]

    write(0, fresh1)
    top3()
    g3, g4 = top4()

    t3, t4 = jnp.transpose(g3), jnp.transpose(g4)
    qw, qp, qq = (block(g4, i) for i in range(3))
    wq, pq = tblock(t4, 0), tblock(t4, 1)
    column_y = jnp.concatenate([block(g3, 0), tblock(t3, 1), tblock(t3, 2), ww * shrink, qw * shrink], axis=0)
    column_w = jnp.concatenate([block(g3, 1), ww, qw, nw, pw], axis=0)
    column_q = jnp.concatenate([block(g3, 2), wq, qq, wp, pq], axis=0)
    column_n = jnp.concatenate([ww * shrink, wn, pw, nn, pn], axis=0)
    column_p = jnp.concatenate([wq * shrink, wp, qp, np_, pp], axis=0)
    gram = jnp.concatenate([column_y, column_w, column_q, column_n, column_p], axis=1)
    product = dot3(work2, gram)
    on_newer = iota((32, 160), 1) // 32 == 3
    resid2 = work2 - dot3(dot3_t(product, fresh1), fresh1) - jnp.where(on_newer, product, 0.0)
    lower2, inverse2 = factor_and_inverse(dot3_t(dot3(resid2, gram), resid2))
    fac_ref[1] = lower2
    write(1, dot3(inverse2, resid2))


def shards(n_gx, n_gy, positions, block_prev, block_cur, neighbours, counts, x_lists, y_lists, w_radial, w_vector, w_mix, w_out):
    n_z, plane = n_gx // 2, 2 * n_gy
    rpd = 32 // plane
    total_rows = 3.0 * ATOMS * n_gx * n_gy
    vmem = pl.BlockSpec(memory_space=pltpu.VMEM)
    blocks, factors = pl.pallas_call(
        functools.partial(kernel, n_gx, n_gy, total_rows),
        out_shape=(
            jax.ShapeDtypeStruct((2, 3, VECTORS, ATOMS), F32),
            jax.ShapeDtypeStruct((2, VECTORS, VECTORS), F32),
        ),
        in_specs=[vmem] * 11,
        out_specs=(vmem, vmem),
        scratch_shapes=[
            pltpu.VMEM((9, 8, 128), F32),
            pltpu.VMEM((9, 48, 128), F32),
            pltpu.VMEM((9, 48, 128), F32),
            pltpu.VMEM((9, 48, 128), F32),
            pltpu.VMEM((3, 9, 48, 128), F32),
            pltpu.VMEM((3, 9, 48, 128), F32),
            pltpu.VMEM((GROUPS, EXTENDED, 256), BF16),
            pltpu.VMEM((RAW, EXTENDED), BF16),
            pltpu.VMEM((HALF_GROUPS, 32, 128), F32),
            pltpu.VMEM((HALF_GROUPS, 16, 128), F32),
            pltpu.VMEM((HALF_GROUPS, 3, 4, 8, 128), F32),
            pltpu.VMEM((2, 32, 8, 128), F32),
            pltpu.VMEM((4, 32, 8, 128), F32),
            pltpu.VMEM((32, 32, 128), F32),
            pltpu.VMEM((160, 192), F32),
            pltpu.VMEM((2, 32, 2, 128), F32),
            pltpu.VMEM((2, plane, rpd, 2, 128), F32),
            pltpu.VMEM((2, n_z, rpd, 2, 128), F32),
            pltpu.VMEM((2, 32, 2, 128), F32),
            pltpu.SemaphoreType.DMA((7, 9)),
            pltpu.SemaphoreType.DMA((7, 9)),
            pltpu.SemaphoreType.DMA((6, 32)),
            pltpu.SemaphoreType.DMA((6, 32)),
        ],
        compiler_params=pltpu.CompilerParams(collective_id=0, has_side_effects=True),
    )(
        positions,
        jnp.transpose(block_prev, (1, 0, 2)),
        jnp.transpose(block_cur, (1, 0, 2)),
        neighbours,
        counts.reshape(1, ATOMS),
        x_lists,
        y_lists,
        w_radial,
        w_vector,
        w_mix,
        w_out.reshape(1, 128),
    )
    return jnp.transpose(blocks, (0, 2, 1, 3)), factors


def solution(mesh):
    placed = (
        P(None, ("gx", "gy")),
        P(None, None, ("gx", "gy")),
        P(None, None, ("gx", "gy")),
        P(None, ("gx", "gy")),
        P(("gx", "gy")),
        P(("gx", "gy"), None, None),
        P(("gx", "gy"), None, None),
        P(),
        P(),
        P(),
        P(),
    )
    return jax.shard_map(
        functools.partial(shards, mesh.shape["gx"], mesh.shape["gy"]),
        mesh=mesh,
        in_specs=placed,
        out_specs=(P(None, None, None, ("gx", "gy")), P()),
        check_vma=False,
    )
```

```python
import functools

import jax
import jax.numpy as jnp
from jax import lax
from jax.experimental import pallas as pl
from jax.experimental.pallas import tpu as pltpu
from jax.sharding import PartitionSpec as P

MESH = pl.DeviceIdType.MESH
F32 = jnp.float32
BF16 = jnp.bfloat16
HIGHEST = lax.Precision.HIGHEST

VECTORS = 32
SLOTS = 32
ATOMS = 64
EXTENDED = 320
RAW = 576
SOFTEN = 0.25
CUTOFF = 5.0
BASIS_SIZE = 8
GROUPS = SLOTS // 4
HALF_GROUPS = 2 * GROUPS
PIVOTS = 4

EX_NEWER, EX_OLDER, EX_FOLD_W, EX_WORK, EX_FOLD_Q, EX_FOLD_Y, EX_META = range(7)


def split2(x):
    high = x.astype(BF16)
    low = (x - high.astype(F32)).astype(BF16)
    return high, low


def mm(a, b):
    return jnp.dot(a, b, preferred_element_type=F32)


def mm_t(a, b):
    return lax.dot_general(a, b, (((1,), (1,)), ((), ())), preferred_element_type=F32)


def dot3(a, b):
    a_high, a_low = split2(a)
    b_high, b_low = split2(b)
    return mm(a_high, b_high) + (mm(a_high, b_low) + mm(a_low, b_high))


def dot3_t(a, b):
    a_high, a_low = split2(a)
    b_high, b_low = split2(b)
    return mm_t(a_high, b_high) + (mm_t(a_high, b_low) + mm_t(a_low, b_high))


def exact(a, b):
    return jnp.dot(a, b, precision=HIGHEST, preferred_element_type=F32)


def iota(shape, axis):
    return lax.broadcasted_iota(jnp.int32, shape, axis)


def factor_and_inverse(gram):
    n = gram.shape[0]
    row, column = iota((n, n), 0), iota((n, n), 1)
    wide_row = iota((n, 2 * n), 0)
    state = jnp.concatenate([gram, (row == column).astype(F32)], axis=1)
    lower = jnp.zeros((n, n), F32)
    for j in range(0, n, PIVOTS):
        at = [slice(j + p, j + p + 1) for p in range(PIVOTS)]
        small, scale, rows, columns = [], [], [], []
        for p in range(PIVOTS):
            entries = []
            for q in range(p):
                entry = state[at[p], at[q]]
                for m in range(q):
                    entry = entry - entries[m] * small[q][m]
                entries.append(entry * scale[q])
            pivot = state[at[p], at[p]]
            for m in range(p):
                pivot = pivot - entries[m] * entries[m]
            small.append(entries)
            scale.append(lax.rsqrt(pivot))
        for p in range(PIVOTS):
            pivot_row, pivot_column = state[at[p], :], state[:, at[p]]
            for m in range(p):
                pivot_row = pivot_row - small[p][m] * rows[m]
                pivot_column = pivot_column - small[p][m] * columns[m]
            rows.append(pivot_row * scale[p])
            columns.append(pivot_column * scale[p])
        below = state
        for p in range(PIVOTS):
            below = below - columns[p] * rows[p]
            lower = jnp.where((column == j + p) & (row >= j + p), columns[p], lower)
        state = jnp.where(wide_row >= j + PIVOTS, below, state)
        for p in range(PIVOTS):
            state = jnp.where(wide_row == j + p, rows[p], state)
    return lower, state[:, n:]


def kernel(
    n_gx,
    n_gy,
    total_rows,
    pos_ref,
    prev_ref,
    cur_ref,
    nb_ref,
    cnt_ref,
    xl_ref,
    yl_ref,
    wr_ref,
    wv_ref,
    wmix_ref,
    wout_ref,
    out_ref,
    fac_ref,
    recv_m,
    recv_n,
    recv_p,
    recv_w,
    fold_send,
    fold_recv,
    d_ref,
    sel_ref,
    fe_ref,
    ms_ref,
    mv_ref,
    dd_ref,
    cf_ref,
    g_ref,
    z_ref,
    pay_ref,
    rs_ref,
    zs_ref,
    tot_ref,
    ex_send,
    ex_recv,
    ar_send,
    ar_recv,
):
    n_z = n_gx // 2
    plane = 2 * n_gy
    rpd = 32 // plane
    gx = lax.axis_index("gx")
    gy = lax.axis_index("gy")
    z_pos, core = gx // 2, gx % 2
    me = gy * 2 + core

    def wrapped(value, size):
        return jnp.where(value >= size, value - size, value)

    gx_near = (wrapped(gx + (n_gx - 1), n_gx), gx, wrapped(gx + 1, n_gx))
    gy_near = (wrapped(gy + (n_gy - 1), n_gy), gy, wrapped(gy + 1, n_gy))
    others = [i for i in range(9) if i != 4]

    def near(i):
        return gx_near[i // 3], gy_near[i % 3]

    def plane_peer(dy, flip):
        to_y = wrapped(gy + dy, n_gy)
        to_core = 1 - core if flip else core
        return to_y * 2 + to_core, (z_pos * 2 + to_core, to_y)

    def line_peer(dz):
        return wrapped(z_pos + dz, n_z) * 2 + core, gy

    def each_plane(act):
        act(0, True)

        def body(d, c):
            dy = d + n_gy // 2
            dy = jnp.where(dy >= n_gy, dy - (n_gy - 1), dy)
            act(dy, False)
            act(dy, True)
            return c

        lax.fori_loop(1, n_gy, body, 0)

    def each_line(act):
        def body(d, c):
            dz = d + n_z // 2 - 1
            dz = jnp.where(dz >= n_z, dz - (n_z - 1), dz)
            act(dz)
            return c

        lax.fori_loop(1, n_z, body, 0)

    barrier = pltpu.get_barrier_semaphore()

    def greet(device):
        pl.semaphore_signal(barrier, inc=1, device_id=device, device_id_type=MESH)

    for i in others:
        greet(near(i))
    each_line(lambda dz: greet(line_peer(dz)))
    each_plane(lambda dy, flip: greet(plane_peer(dy, flip)[1]))

    def pack_own(source, target):
        for c in range(3):
            block = source[c]
            target[4, c * 16 : (c + 1) * 16, :] = jnp.concatenate([block[:16], block[16:]], axis=1)

    pack_own(cur_ref, recv_n)
    pack_own(prev_ref, recv_p)
    left = jnp.concatenate([pos_ref[...], jnp.zeros((5, ATOMS), F32)], axis=0)
    right = jnp.concatenate(
        [xl_ref[0].astype(F32), yl_ref[0].astype(F32), jnp.zeros((4, ATOMS), F32)], axis=0
    )
    recv_m[4] = jnp.concatenate([left, right], axis=1)

    pl.semaphore_wait(barrier, 8 + (n_z - 1) + (plane - 1))

    def spread_copy(number, ref, i):
        return pltpu.make_async_remote_copy(
            src_ref=ref.at[4],
            dst_ref=ref.at[8 - i],
            send_sem=ex_send.at[number, i],
            recv_sem=ex_recv.at[number, 8 - i],
            device_id=near(i),
            device_id_type=MESH,
        )

    def fold_copy(number, slot, i):
        return pltpu.make_async_remote_copy(
            src_ref=fold_send.at[slot, i],
            dst_ref=fold_recv.at[slot, 8 - i],
            send_sem=ex_send.at[number, i],
            recv_sem=ex_recv.at[number, 8 - i],
            device_id=near(i),
            device_id_type=MESH,
        )

    def start_all(make):
        for i in others:
            make(i).start()

    def wait_all(make):
        for i in others:
            make(i).wait()

    meta = functools.partial(spread_copy, EX_META, recv_m)
    newer = functools.partial(spread_copy, EX_NEWER, recv_n)
    older = functools.partial(spread_copy, EX_OLDER, recv_p)
    work = functools.partial(spread_copy, EX_WORK, recv_w)
    fold_w = functools.partial(fold_copy, EX_FOLD_W, 0)
    fold_q = functools.partial(fold_copy, EX_FOLD_Q, 1)
    fold_y = functools.partial(fold_copy, EX_FOLD_Y, 2)
    start_all(meta)
    start_all(newer)
    start_all(older)

    count_row = cnt_ref[...]
    count_row = jnp.concatenate([count_row] * 4, axis=1)
    lane = iota((1, 256), 1)

    def build_incidence(g, c):
        rows = [nb_ref[pl.ds(4 * g + s, 1), :] for s in range(4)]
        index = jnp.concatenate(rows, axis=1)
        valid = (4 * g + lane // ATOMS) < count_row
        index = jnp.where(valid, index, -1)
        own = jnp.where(valid, lane % ATOMS, -1)
        picked = (iota((EXTENDED, 256), 0) == index).astype(F32)
        minus = (iota((ATOMS, 256), 0) == own).astype(F32)
        d_ref[g] = jnp.concatenate([picked[:ATOMS] - minus, picked[ATOMS:]], axis=0).astype(BF16)
        return c

    lax.fori_loop(0, GROUPS, build_incidence, 0)

    w_vec = wv_ref[...]
    w_rad = wr_ref[...]
    w_mix = wmix_ref[...]
    w_mix_t = jnp.transpose(w_mix)
    pad = jnp.zeros((112, 128), F32)
    w_both_t = jnp.transpose(jnp.concatenate([w_rad, w_vec, pad], axis=0))
    w_rad_t = w_both_t[:, :8]
    w_vec_t = w_both_t[:, 8:16]
    w_out_t = jnp.transpose(jnp.broadcast_to(wout_ref[...], (128, 128)))
    level = jnp.sqrt(jnp.sum(wout_ref[...] * wout_ref[...])) * jnp.sqrt(jnp.sum(w_mix * w_mix)) * jnp.sum(w_vec * w_vec)
    shrink = 1.0 / jnp.clip(level, 1e-8, 1e8)
    grow = jnp.clip(level, 1e-8, 1e8)

    def raw_rows(ref):
        pieces = []
        for c in range(3):
            for h in range(2):
                pieces.append(
                    jnp.concatenate(
                        [ref[i, c * 16 : (c + 1) * 16, h * ATOMS : (h + 1) * ATOMS] for i in range(9)], axis=1
                    )
                )
        return jnp.concatenate(pieces, axis=0)

    def extend(ref):
        high, low = split2(raw_rows(ref))
        return mm(jnp.concatenate([high, low], axis=0), sel_ref[...]).astype(BF16)

    wait_all(meta)

    def listed(slot, row):
        return recv_m[slot, row : row + 1, ATOMS:]

    own_row = iota((1, ATOMS), 1).astype(F32)

    def widened(own_slot, left_slot, right_slot):
        return jnp.concatenate(
            [own_row + own_slot * 64.0, listed(left_slot, 0) + left_slot * 64.0, listed(right_slot, 1) + right_slot * 64.0],
            axis=1,
        )

    def looked_up(table, picks):
        hot = (iota((3 * ATOMS, ATOMS), 0).astype(F32) == picks).astype(F32)
        return exact(jnp.broadcast_to(table, (8, 3 * ATOMS)), hot)[0:1]

    before = looked_up(widened(3, 0, 6), listed(3, 2))
    after = looked_up(widened(5, 2, 8), listed(5, 3))
    to_raw = jnp.concatenate([widened(4, 1, 7), before, after], axis=1)
    to_raw = (to_raw + 0.5).astype(jnp.int32)
    sel_ref[...] = (iota((RAW, EXTENDED), 0) == to_raw).astype(F32).astype(BF16)

    raw_pos = jnp.concatenate([recv_m[i, :, :ATOMS] for i in range(9)], axis=1)
    p_high = raw_pos.astype(BF16)
    rest = raw_pos - p_high.astype(F32)
    p_mid = rest.astype(BF16)
    p_low = (rest - p_mid.astype(F32)).astype(BF16)
    zero8 = jnp.zeros((8, RAW), BF16)
    pos_ext = mm(jnp.concatenate([p_high, p_mid, p_low, zero8], axis=0), sel_ref[...]).astype(BF16)

    center = CUTOFF * (iota((BASIS_SIZE, 1), 0).astype(F32) + 0.5) / BASIS_SIZE
    descriptor = [jnp.zeros((BASIS_SIZE, 256), F32) for _ in range(4)]

    def edge_rows(g):
        parts = mm(pos_ext, d_ref[g])
        d = parts[0:8] + (parts[8:16] + parts[16:24])
        d = d[0:3]
        squared = jnp.sum(d * d, axis=0, keepdims=True) + SOFTEN
        inv_r = lax.rsqrt(squared)
        r = squared * inv_r
        h = d * inv_r
        q = jnp.maximum(1.0 - squared * (1.0 / (CUTOFF * CUTOFF)), 0.0)
        env = q * q * q
        env1 = (-6.0 / 25.0) * r * q * q
        env2 = (-6.0 / 25.0) * q * q + (24.0 / 625.0) * squared * q
        offset = r - center
        bell = jnp.exp(-2.0 * offset * offset)
        f = bell * env
        f1 = bell * (env1 - 4.0 * offset * env)
        f2 = bell * (env2 - 8.0 * offset * env1 + (16.0 * offset * offset - 4.0) * env)
        return d, h, inv_r, f, f1, f2

    def first_pass(g, descriptor):
        d, h, inv_r, f, f1, f2 = edge_rows(g)
        valid = ((4 * g + lane // ATOMS) < count_row).astype(F32)
        e = f1 - f * inv_r
        for half in range(2):
            cut = slice(half * 128, (half + 1) * 128)
            fe_ref[2 * g + half, 0:8, :] = f[:, cut]
            fe_ref[2 * g + half, 8:16, :] = f1[:, cut]
            fe_ref[2 * g + half, 16:24, :] = e[:, cut]
            ms_ref[2 * g + half, 0:3, :] = h[:, cut]
            ms_ref[2 * g + half, 3:4, :] = inv_r[:, cut]
            fe_ref[2 * g + half, 24:32, :] = f2[:, cut]
        masked = f * valid
        return (
            descriptor[0] + masked,
            descriptor[1] + masked * h[0:1],
            descriptor[2] + masked * h[1:2],
            descriptor[3] + masked * h[2:3],
        )

    descriptor = lax.fori_loop(0, GROUPS, first_pass, tuple(descriptor), unroll=True)

    def fold_lanes(x):
        x = x[:, :128] + x[:, 128:]
        return x + pltpu.roll(x, 64, 1)

    descriptor = [fold_lanes(x) for x in descriptor]

    v = [dot3(w_vec_t, descriptor[c + 1]) for c in range(3)]
    mixed_in = dot3(w_rad_t, descriptor[0]) + (v[0] * v[0] + v[1] * v[1] + v[2] * v[2])
    x = dot3(w_mix_t, mixed_in)
    gate = jax.nn.sigmoid(x)
    slope = gate * (1.0 - gate)
    silu1 = gate + x * slope
    silu2 = slope * (2.0 + x * (1.0 - 2.0 * gate))
    grad_m = dot3(w_mix, w_out_t * silu1)
    bend = w_out_t * silu2
    coeffs = [dot3(w_rad, grad_m)] + [dot3(w_vec, 2.0 * v[c] * grad_m) for c in range(3)]

    low_lane = iota((1, 128), 1) < 64
    w_rad_hl = split2(w_rad)
    w_vec_hl = split2(w_vec)
    mix_hl = split2(w_mix)
    mix_t_hl = split2(w_mix_t)

    def dot_pre(a, b):
        b_high, b_low = split2(b)
        rows = a[0].shape[0]
        both = mm(jnp.concatenate(a, axis=0), b_high)
        return both[:rows] + (both[rows:] + mm(a[0], b_low))

    for kind in range(4):
        table = w_rad_t if kind == 0 else w_vec_t
        columns = [jnp.where(low_lane, table[:, 2 * m : 2 * m + 1], table[:, 2 * m + 1 : 2 * m + 2]) for m in range(4)]
        base = columns if kind == 0 else [2.0 * v[kind - 1] * column for column in columns]
        moved = jnp.concatenate(base, axis=1)
        bend4 = jnp.concatenate([bend] * 4, axis=1)
        shift = dot_pre(mix_hl, bend4 * dot_pre(mix_t_hl, moved))
        parts = [dot_pre(w_rad_hl, shift)]
        for c in range(3):
            term = jnp.concatenate([2.0 * v[c]] * 4, axis=1) * shift
            if kind == c + 1:
                term = term + jnp.concatenate([2.0 * grad_m * column for column in columns], axis=1)
            parts.append(dot_pre(w_vec_hl, term))
        block = jnp.concatenate(parts, axis=0)
        for m in range(4):
            piece = block[:, m * 128 : (m + 1) * 128]
            turned = pltpu.roll(piece, 64, 1)
            g_ref[kind * 8 + 2 * m] = jnp.where(low_lane, piece, turned)
            g_ref[kind * 8 + 2 * m + 1] = jnp.where(low_lane, turned, piece)

    def second_pass(hg, c):
        f, f1, f2 = fe_ref[hg, 0:8, :], fe_ref[hg, 8:16, :], fe_ref[hg, 24:32, :]
        h = [ms_ref[hg, b : b + 1, :] for b in range(3)]
        inv_r = ms_ref[hg, 3:4, :]
        r = 1.0 / inv_r

        def total(coeff, values):
            return jnp.sum(coeff * values, axis=0, keepdims=True)

        s2 = total(coeffs[0], f2)
        s1 = total(coeffs[0], f1)
        for b in range(3):
            psi, psi1, psi2 = (total(coeffs[b + 1], values) for values in (f, f1, f2))
            chi1 = (psi1 - psi * inv_r) * inv_r
            chi2 = (psi2 - 2.0 * chi1) * inv_r
            d_b = h[b] * r
            s2 = s2 + d_b * chi2
            s1 = s1 + d_b * chi1
            ms_ref[hg, 6 + b : 7 + b, :] = chi1
        s1 = s1 * inv_r
        ms_ref[hg, 4:5, :] = s2 - s1
        ms_ref[hg, 5:6, :] = s1
        return c

    lax.fori_loop(0, HALF_GROUPS, second_pass, 0, unroll=True)

    def wide(row):
        return jnp.broadcast_to(row, (8, 128))

    def change_of(ext):
        def gather(g, c):
            moved = mm(ext, d_ref[g])
            moved = moved[:96] + moved[96:]
            mv_ref[2 * g] = moved[:, :128].reshape(3, 4, 8, 128)
            mv_ref[2 * g + 1] = moved[:, 128:].reshape(3, 4, 8, 128)
            return c

        lax.fori_loop(0, GROUPS, gather, 0, unroll=True)

        def pair(p, c):
            for part in range(2):

                def edges(hg, acc):
                    h = [wide(ms_ref[hg, b : b + 1, :]) for b in range(3)]
                    inv_r = wide(ms_ref[hg, 3:4, :])
                    new = list(acc)
                    scaled, along, rho = [], [], []
                    for t in range(2):
                        u = [mv_ref[hg, b, 2 * p + t] for b in range(3)]
                        rho.append(h[0] * u[0] + h[1] * u[1] + h[2] * u[2])
                        scaled.append([u[b] * inv_r for b in range(3)])
                        along.append([h[b] * rho[t] for b in range(3)])
                    for k in range(4):
                        row = 4 * part + k
                        f = wide(fe_ref[hg, row : row + 1, :])
                        f1 = wide(fe_ref[hg, 8 + row : 9 + row, :])
                        e = wide(fe_ref[hg, 16 + row : 17 + row, :])
                        for t in range(2):
                            new[16 * t + k] = acc[16 * t + k] + f1 * rho[t]
                            for b in range(3):
                                at = 16 * t + 4 * (b + 1) + k
                                new[at] = acc[at] + (f * scaled[t][b] + e * along[t][b])
                    return tuple(new)

                acc = lax.fori_loop(
                    0, HALF_GROUPS, edges, tuple(jnp.zeros((8, 128), F32) for _ in range(32)), unroll=4
                )
                for at in range(16):
                    first, second = acc[at], acc[16 + at]
                    first = first + pltpu.roll(first, 64, 1)
                    second = second + pltpu.roll(second, 64, 1)
                    dd_ref[p, 8 * (at // 4) + 4 * part + at % 4] = jnp.where(low_lane, first, second)
            return c

        lax.fori_loop(0, 2, pair, 0)

    def response():
        def pair(p, c):
            def one(j, acc):
                delta = dd_ref[p, j]
                return tuple(acc[i] + wide(g_ref[j, i : i + 1, :]) * delta for i in range(32))

            acc = lax.fori_loop(0, 32, one, tuple(jnp.zeros((8, 128), F32) for _ in range(32)), unroll=4)
            for i in range(32):
                turned = pltpu.roll(acc[i], 64, 1)
                cf_ref[2 * p, i] = jnp.where(low_lane, acc[i], turned)
                cf_ref[2 * p + 1, i] = jnp.where(low_lane, turned, acc[i])
            return c

        lax.fori_loop(0, 2, pair, 0)

    def forces(slot):
        def tile(tt, c):
            a = [cf_ref[tt, i] for i in range(32)]

            def edges(hg, c2):
                u = [mv_ref[hg, b, tt] for b in range(3)]
                h = [wide(ms_ref[hg, b : b + 1, :]) for b in range(3)]
                inv_r = wide(ms_ref[hg, 3:4, :])
                alpha = wide(ms_ref[hg, 4:5, :])
                beta = wide(ms_ref[hg, 5:6, :])
                chi = [wide(ms_ref[hg, 6 + b : 7 + b, :]) for b in range(3)]
                rho = h[0] * u[0] + h[1] * u[1] + h[2] * u[2]
                level = alpha * rho + (chi[0] * u[0] + chi[1] * u[1] + chi[2] * u[2])
                across = [None] * 3
                along = [None] * 3
                for k in range(8):
                    f = wide(fe_ref[hg, k : k + 1, :])
                    f1 = wide(fe_ref[hg, 8 + k : 9 + k, :])
                    e = wide(fe_ref[hg, 16 + k : 17 + k, :])
                    level = level + f1 * a[k]
                    for b in range(3):
                        coeff = a[8 * (b + 1) + k]
                        across[b] = f * coeff if k == 0 else across[b] + f * coeff
                        along[b] = e * coeff if k == 0 else along[b] + e * coeff
                level = level + (h[0] * along[0] + h[1] * along[1] + h[2] * along[2])
                for b in range(3):
                    mv_ref[hg, b, tt] = inv_r * across[b] + beta * u[b] + h[b] * level + chi[b] * rho
                return c2

            lax.fori_loop(0, HALF_GROUPS, edges, 0, unroll=4)
            return c

        lax.fori_loop(0, 4, tile, 0)

        def scatter(g, acc):
            edge = jnp.concatenate([mv_ref[2 * g].reshape(96, 128), mv_ref[2 * g + 1].reshape(96, 128)], axis=1)
            high, low = split2(edge)
            return acc + mm_t(jnp.concatenate([high, low], axis=0), d_ref[g])

        both = lax.fori_loop(0, GROUPS, scatter, jnp.zeros((192, EXTENDED), F32), unroll=True)
        high, low = split2(both[:96] + both[96:])
        raw = mm_t(jnp.concatenate([high, low], axis=0), sel_ref[...])
        raw = raw[:96] + raw[96:]
        for i in range(9):
            part = raw[:, i * ATOMS : (i + 1) * ATOMS]
            for c in range(3):
                top, bottom = part[c * 32 : c * 32 + 16], part[c * 32 + 16 : c * 32 + 32]
                fold_send[slot, i, c * 16 : (c + 1) * 16, :] = jnp.concatenate([top, bottom], axis=1)

    def folded(slot):
        total = fold_send[slot, 4]
        for i in range(9):
            if i != 4:
                total = total + fold_recv[slot, i]
        return total

    def keep_rows(at, packed):
        for h in range(2):
            z_ref[at + h * 16 : at + h * 16 + 16, :] = jnp.concatenate(
                [packed[c * 16 : (c + 1) * 16, h * ATOMS : (h + 1) * ATOMS] for c in range(3)], axis=1
            )

    def reduce_steps(n):
        def slice_of(ref, r):
            return ref.at[n, pl.ds(r * rpd, rpd)]

        def stage0(dy, flip):
            peer, device = plane_peer(dy, flip)
            slot = 2 * dy + int(flip)
            return pltpu.make_async_remote_copy(
                src_ref=slice_of(pay_ref, peer),
                dst_ref=rs_ref.at[n, me],
                send_sem=ar_send.at[3 * n, slot],
                recv_sem=ar_recv.at[3 * n, slot],
                device_id=device,
                device_id_type=MESH,
            )

        def stage1(dz):
            return pltpu.make_async_remote_copy(
                src_ref=zs_ref.at[n, z_pos],
                dst_ref=zs_ref.at[n, z_pos],
                send_sem=ar_send.at[3 * n + 1, dz],
                recv_sem=ar_recv.at[3 * n + 1, dz],
                device_id=line_peer(dz),
                device_id_type=MESH,
            )

        def stage2(dy, flip):
            slot = 2 * dy + int(flip)
            return pltpu.make_async_remote_copy(
                src_ref=slice_of(tot_ref, me),
                dst_ref=slice_of(tot_ref, me),
                send_sem=ar_send.at[3 * n + 2, slot],
                recv_sem=ar_recv.at[3 * n + 2, slot],
                device_id=plane_peer(dy, flip)[1],
                device_id_type=MESH,
            )

        def begin(make, each):
            each(lambda *peer: make(*peer).start())

        def end(make, each):
            each(lambda *peer: make(*peer).wait())

        def first():
            begin(stage0, each_plane)
            rs_ref[n, me] = pay_ref[n, pl.ds(me * rpd, rpd)]

        def second():
            end(stage0, each_plane)
            zs_ref[n, z_pos] = jnp.sum(rs_ref[n], axis=0)
            begin(stage1, each_line)

        def third():
            end(stage1, each_line)
            tot_ref[n, pl.ds(me * rpd, rpd)] = jnp.sum(zs_ref[n], axis=0) * (1.0 / total_rows)
            begin(stage2, each_plane)

        def last():
            end(stage2, each_plane)
            return tot_ref[n, :, 0, :], tot_ref[n, :, 1, :]

        return first, second, third, last

    def rows_of(at):
        return z_ref[at : at + 32, :]

    none = jnp.zeros((32, 192), F32)
    low1, low2, low3, low4 = reduce_steps(0)
    top1, top2, top3, top4 = reduce_steps(1)

    wait_all(newer)
    change_of(extend(recv_n))
    response()
    forces(0)
    start_all(fold_w)

    wait_all(older)
    change_of(extend(recv_p))
    response()
    keep_rows(96, recv_n[4])
    keep_rows(128, recv_p[4])
    n_rows, p_rows = rows_of(96), rows_of(128)
    pay_ref[0, :, 1, :] = dot3_t(n_rows, jnp.concatenate([n_rows, p_rows, none, none], axis=0)) + dot3_t(
        p_rows, jnp.concatenate([none, none, p_rows, none], axis=0)
    )

    wait_all(fold_w)
    recv_w[4] = folded(0)
    start_all(work)

    keep_rows(32, recv_w[4])
    w_rows = rows_of(32)
    pay_ref[0, :, 0, :] = dot3_t(w_rows, jnp.concatenate([w_rows, rows_of(96), rows_of(128), none], axis=0))
    low1()
    forces(1)
    start_all(fold_q)
    low2()

    wait_all(work)
    change_of(extend(recv_w))
    response()
    forces(2)
    start_all(fold_y)
    low3()

    wait_all(fold_q)
    keep_rows(64, folded(1))
    q_rows = rows_of(64)
    pay_ref[1, :, 1, :] = dot3_t(q_rows, jnp.concatenate([rows_of(32), rows_of(128), q_rows, none], axis=0))
    wait_all(fold_y)
    keep_rows(0, folded(2) * shrink)
    y_rows = rows_of(0)
    pay_ref[1, :, 0, :] = dot3_t(y_rows, jnp.concatenate([y_rows, rows_of(32), rows_of(64), none], axis=0))
    top1()

    def block(source, i):
        return source[:, i * 32 : (i + 1) * 32]

    def tblock(source, i):
        return source[i * 32 : (i + 1) * 32]

    g1, g2 = low4()
    t1, t2 = jnp.transpose(g1), jnp.transpose(g2)
    eye = (iota((32, 32), 0) == iota((32, 32), 1)).astype(F32)
    zero = jnp.zeros((32, 32), F32)
    ww, wn, wp = (block(g1, i) for i in range(3))
    nw, pw, pn = tblock(t1, 1), tblock(t1, 2), tblock(t2, 1)
    nn, np_, pp = (block(g2, i) for i in range(3))
    small = jnp.concatenate(
        [
            jnp.concatenate([ww, nw, pw], axis=0),
            jnp.concatenate([wn, nn, pn], axis=0),
            jnp.concatenate([wp, np_, pp], axis=0),
        ],
        axis=1,
    )
    resid1 = jnp.concatenate([eye, -wn, -wp], axis=1)
    lower1, inverse1 = factor_and_inverse(dot3_t(dot3(resid1, small), resid1))
    fac_ref[0] = lower1
    fresh1 = dot3(inverse1, resid1)
    f_w, f_n, f_p = (block(fresh1, i) for i in range(3))
    fresh1 = jnp.concatenate([zero, f_w, zero, f_n, f_p], axis=1)
    work2 = jnp.concatenate([inverse1 * grow, f_n, f_p, zero, zero], axis=1)
    top2()

    def write(s, coefficients):
        fresh = dot3(coefficients, z_ref[...])
        for c in range(3):
            out_ref[s, c] = fresh[:, c * ATOMS : (c + 1) * ATOMS]

    write(0, fresh1)
    top3()
    g3, g4 = top4()

    t3, t4 = jnp.transpose(g3), jnp.transpose(g4)
    qw, qp, qq = (block(g4, i) for i in range(3))
    wq, pq = tblock(t4, 0), tblock(t4, 1)
    column_y = jnp.concatenate([block(g3, 0), tblock(t3, 1), tblock(t3, 2), ww * shrink, qw * shrink], axis=0)
    column_w = jnp.concatenate([block(g3, 1), ww, qw, nw, pw], axis=0)
    column_q = jnp.concatenate([block(g3, 2), wq, qq, wp, pq], axis=0)
    column_n = jnp.concatenate([ww * shrink, wn, pw, nn, pn], axis=0)
    column_p = jnp.concatenate([wq * shrink, wp, qp, np_, pp], axis=0)
    gram = jnp.concatenate([column_y, column_w, column_q, column_n, column_p], axis=1)
    product = dot3(work2, gram)
    on_newer = iota((32, 160), 1) // 32 == 3
    resid2 = work2 - dot3(dot3_t(product, fresh1), fresh1) - jnp.where(on_newer, product, 0.0)
    lower2, inverse2 = factor_and_inverse(dot3_t(dot3(resid2, gram), resid2))
    fac_ref[1] = lower2
    write(1, dot3(inverse2, resid2))


def shards(n_gx, n_gy, positions, block_prev, block_cur, neighbours, counts, x_lists, y_lists, w_radial, w_vector, w_mix, w_out):
    n_z, plane = n_gx // 2, 2 * n_gy
    rpd = 32 // plane
    total_rows = 3.0 * ATOMS * n_gx * n_gy
    vmem = pl.BlockSpec(memory_space=pltpu.VMEM)
    blocks, factors = pl.pallas_call(
        functools.partial(kernel, n_gx, n_gy, total_rows),
        out_shape=(
            jax.ShapeDtypeStruct((2, 3, VECTORS, ATOMS), F32),
            jax.ShapeDtypeStruct((2, VECTORS, VECTORS), F32),
        ),
        in_specs=[vmem] * 11,
        out_specs=(vmem, vmem),
        scratch_shapes=[
            pltpu.VMEM((9, 8, 128), F32),
            pltpu.VMEM((9, 48, 128), F32),
            pltpu.VMEM((9, 48, 128), F32),
            pltpu.VMEM((9, 48, 128), F32),
            pltpu.VMEM((3, 9, 48, 128), F32),
            pltpu.VMEM((3, 9, 48, 128), F32),
            pltpu.VMEM((GROUPS, EXTENDED, 256), BF16),
            pltpu.VMEM((RAW, EXTENDED), BF16),
            pltpu.VMEM((HALF_GROUPS, 32, 128), F32),
            pltpu.VMEM((HALF_GROUPS, 16, 128), F32),
            pltpu.VMEM((HALF_GROUPS, 3, 4, 8, 128), F32),
            pltpu.VMEM((2, 32, 8, 128), F32),
            pltpu.VMEM((4, 32, 8, 128), F32),
            pltpu.VMEM((32, 32, 128), F32),
            pltpu.VMEM((160, 192), F32),
            pltpu.VMEM((2, 32, 2, 128), F32),
            pltpu.VMEM((2, plane, rpd, 2, 128), F32),
            pltpu.VMEM((2, n_z, rpd, 2, 128), F32),
            pltpu.VMEM((2, 32, 2, 128), F32),
            pltpu.SemaphoreType.DMA((7, 9)),
            pltpu.SemaphoreType.DMA((7, 9)),
            pltpu.SemaphoreType.DMA((6, 32)),
            pltpu.SemaphoreType.DMA((6, 32)),
        ],
        compiler_params=pltpu.CompilerParams(collective_id=0, has_side_effects=True),
    )(
        positions,
        jnp.transpose(block_prev, (1, 0, 2)),
        jnp.transpose(block_cur, (1, 0, 2)),
        neighbours,
        counts.reshape(1, ATOMS),
        x_lists,
        y_lists,
        w_radial,
        w_vector,
        w_mix,
        w_out.reshape(1, 128),
    )
    return jnp.transpose(blocks, (0, 2, 1, 3)), factors


def solution(mesh):
    placed = (
        P(None, ("gx", "gy")),
        P(None, None, ("gx", "gy")),
        P(None, None, ("gx", "gy")),
        P(None, ("gx", "gy")),
        P(("gx", "gy")),
        P(("gx", "gy"), None, None),
        P(("gx", "gy"), None, None),
        P(),
        P(),
        P(),
        P(),
    )
    return jax.shard_map(
        functools.partial(shards, mesh.shape["gx"], mesh.shape["gy"]),
        mesh=mesh,
        in_specs=placed,
        out_specs=(P(None, None, None, ("gx", "gy")), P()),
        check_vma=False,
    )
```
